128 devices in a mesh: row: 8 (over z, y_lo), col: 16 (over x, y_hi, core).
Axes of the slice: x: 4, y: 4 (y_hi: 2, y_lo: 2; y = y_hi * 2 + y_lo), z: 4, core: 2. Of those that a mesh axis runs over, the one named last changes fastest.
Arguments:
- covariance: float32 [16384, 16384], P('row', 'col'), may hold values from -1 to 3, as said below
- center: float32 [16384], replicated, may hold values from 0.4 to 1
- links: float32 [4, 16384], replicated, may hold values from 0.05 to 0.25
- process: float32 [16384], replicated, may hold values from 0.1 to 1
- wells: int32 [1, 256], replicated, may hold values from 0 to 16383, as said below
- noise: float32 [1, 256], replicated, may hold values from 0.05 to 0.5
Outputs:
- updated: float32 [16384, 16384], P('row', 'col')
The draws below stay inside these ranges and needn't reach their ends.
Inputs may be any that keep to these rules, and one draw needn't show every extreme that they name: `covariance`: symmetric positive definite. `wells`: each row holds 256 distinct cells; at most 32 of them lie in one aligned block of 1024 cells, and exactly 32 in some block.
All inputs are finite; a program needn't handle non-finite values.
Results may differ from the reference program's by a relative error of at most 0.0001.
Values sent between devices are 32-bit elements; how exact they have to be, the bound alone decides.
No kernel may reach another device: no remote copies, remote signals or barrier semaphores. Data moves between devices by JAX's collectives and lax.ppermute only.
A program may use at most 128 MiB of HBM per device.

```python
import math
import jax
import jax.numpy as jnp
from jax import lax

NGX = 128
NGY = 128
M = 256
WMAX = 32
STEPS = 1
NCELL = 16384
CBLK = 1024


def draw_covariance(key, part):
    base = jax.random.normal(key, (NCELL, NCELL), jnp.float32)
    lift = 2.0
    sym = (base + base.T) * (0.5 / math.sqrt(NCELL))
    return sym + lift * jnp.eye(NCELL, dtype=jnp.float32)


def draw_wells(key, part):
    blocks = NCELL // CBLK
    keys = jax.random.split(jax.random.fold_in(key, 11), STEPS * blocks)
    perms = jax.vmap(lambda k: jax.random.permutation(k, CBLK))(keys).reshape(STEPS, blocks, CBLK)
    first = jax.random.randint(jax.random.fold_in(key, 12), (STEPS,), 0, blocks)
    slot = jnp.arange(M, dtype=jnp.int32)
    later = jnp.maximum(slot - WMAX, 0)
    span = max(blocks - 1, 1)
    block = jnp.where(slot[None, :] < WMAX, first[:, None], (first[:, None] + 1 + later[None, :] % span) % blocks)
    rank = jnp.where(slot[None, :] < WMAX, slot[None, :], later[None, :] // span)
    offset = perms[jnp.arange(STEPS, dtype=jnp.int32)[:, None], block, rank]
    cells = (block * CBLK + offset).astype(jnp.int32)
    orders = jax.vmap(lambda k: jax.random.permutation(k, M))(jax.random.split(jax.random.fold_in(key, 13), STEPS))
    return jnp.take_along_axis(cells, orders.astype(jnp.int32), axis=1).astype(jnp.int32)


def setup_inputs(seed: int = 0) -> dict:
    arg_keys = jax.random.split(jax.random.key(seed), 7)
    covariance = draw_covariance(jax.random.fold_in(arg_keys[6], 71), 0)
    center = jnp.clip(jnp.exp(jax.random.uniform(arg_keys[1], (NCELL,), jnp.float32, math.log(0.4), math.log(1.0))), 0.4, 1.0)
    links = jnp.clip(jnp.exp(jax.random.uniform(arg_keys[2], (4, NCELL), jnp.float32, math.log(0.05), math.log(0.25))), 0.05, 0.25)
    process = jnp.clip(jnp.exp(jax.random.uniform(arg_keys[3], (NCELL,), jnp.float32, math.log(0.1), math.log(1.0))), 0.1, 1.0)
    wells = draw_wells(jax.random.fold_in(arg_keys[6], 71), 0)
    noise = jnp.clip(jnp.exp(jax.random.uniform(arg_keys[5], (STEPS, M), jnp.float32, math.log(0.05), math.log(0.5))), 0.05, 0.5)
    return dict(covariance=covariance, center=center, links=links, process=process, wells=wells, noise=noise)


def apply_left(matrix, center, links):
    field = matrix.reshape(NGX, NGY, -1)
    padded = jnp.pad(field, ((1, 1), (1, 1), (0, 0)))
    own = center.reshape(NGX, NGY, 1)
    coef = links.reshape(4, NGX, NGY, 1)
    out = own * field + coef[0] * padded[:-2, 1:-1] + coef[1] * padded[2:, 1:-1]
    out = out + coef[2] * padded[1:-1, :-2] + coef[3] * padded[1:-1, 2:]
    return out.reshape(NCELL, -1)

def apply_right(matrix, center, links):
    field = matrix.reshape(-1, NGX, NGY)
    padded = jnp.pad(field, ((0, 0), (1, 1), (1, 1)))
    own = center.reshape(1, NGX, NGY)
    coef = links.reshape(4, 1, NGX, NGY)
    out = own * field + coef[0] * padded[:, :-2, 1:-1] + coef[1] * padded[:, 2:, 1:-1]
    out = out + coef[2] * padded[:, 1:-1, :-2] + coef[3] * padded[:, 1:-1, 2:]
    return out.reshape(-1, NCELL)

def reference(covariance, center, links, process, wells, noise):
    current = covariance
    diag_index = jnp.arange(NCELL, dtype=jnp.int32)
    for step in range(STEPS):
        left = apply_left(current, center, links)
        predicted = apply_right(left, center, links)
        predicted = predicted.at[diag_index, diag_index].add(process)
        chosen = wells[step]
        strip = jnp.take(predicted, chosen, axis=1)
        across = jnp.take(predicted, chosen, axis=0)
        innovation = jnp.take(strip, chosen, axis=0) + jnp.diag(noise[step])
        factor = jnp.linalg.cholesky(innovation)
        solved = jax.scipy.linalg.cho_solve((factor, True), across)
        current = predicted - jnp.dot(strip, solved, precision=lax.Precision.HIGHEST)
    return current
```

```python
import functools

import jax
import jax.numpy as jnp
from jax import lax
from jax.experimental import pallas as pl
from jax.experimental.pallas import tpu as pltpu
from jax.sharding import PartitionSpec as P

NGY = 128
M = 256
WMAX = 32
ROWS = 8
COLS = 16
HALF = 2 * WMAX
SLOTS = ROWS * HALF
F32 = jnp.float32
BF16 = jnp.bfloat16
HI = lax.Precision.HIGHEST


def cost(flops, size):
    return pl.CostEstimate(flops=flops, bytes_accessed=size, transcendentals=0)


def vmem(count):
    return [pl.BlockSpec(memory_space=pltpu.VMEM)] * count


def rows_kernel(idx, coef, send, p_ref, z_ref, up_ref, dn_ref):
    def one(s, carry):
        i = idx[0, s]
        total = coef[0, s] * p_ref[pl.ds(i, 1), :]
        for k in range(1, 5):
            total = total + coef[k, s] * p_ref[pl.ds(idx[k, s], 1), :]
        z_ref[pl.ds(s, 1), :] = total
        return carry

    lax.fori_loop(0, HALF, one, 0)

    def two(s, carry):
        up_ref[pl.ds(s, 1), :] = p_ref[pl.ds(send[0, s], 1), :]
        dn_ref[pl.ds(s, 1), :] = p_ref[pl.ds(send[1, s], 1), :]
        return carry

    lax.fori_loop(0, WMAX, two, 0)


def well_rows(idx, coef, send, block):
    cols = block.shape[1]
    smem = pl.BlockSpec(memory_space=pltpu.SMEM)
    return pl.pallas_call(
        rows_kernel,
        out_shape=(
            jax.ShapeDtypeStruct((HALF, cols), F32),
            jax.ShapeDtypeStruct((WMAX, cols), F32),
            jax.ShapeDtypeStruct((WMAX, cols), F32),
        ),
        in_specs=[smem, smem, smem] + vmem(1),
        out_specs=tuple(vmem(3)),
        compiler_params=pltpu.CompilerParams(vmem_limit_bytes=24 << 20),
        cost_estimate=cost(10 * HALF * cols, block.size * 4),
        name="well_rows",
    )(idx, coef, send, block)


def across_lanes(parts, coef, lo, hi):
    out = []
    for t in range(lo, hi):
        left, mid, right = parts[t], parts[t + 1], parts[t + 2]
        c = coef[:, t * NGY : (t + 1) * NGY]
        total = c[0:1] * mid + c[1:2] * left + c[2:3] * right
        total = total + c[3:4] * pltpu.roll(mid, 1, 1) + c[4:5] * pltpu.roll(mid, NGY - 1, 1)
        out.append(total)
    return out


def cols_kernel(z_ref, zl_ref, zr_ref, coef_ref, diag_ref, proc_ref, target_ref, x_ref, g_ref):
    cols = z_ref.shape[1]
    tiles = cols // NGY
    parts = [zl_ref[...]] + [z_ref[:, t * NGY : (t + 1) * NGY] for t in range(tiles)] + [zr_ref[...]]
    out = across_lanes(parts, coef_ref[...], 0, tiles)
    x = jnp.concatenate(out, axis=1)
    lane = lax.broadcasted_iota(jnp.int32, x.shape, 1)
    x = x + jnp.where(lane == diag_ref[...], proc_ref[...], 0.0)
    x_ref[...] = x
    pick = lax.broadcasted_iota(jnp.int32, (cols, NGY), 0) == target_ref[...]
    g_ref[...] = jnp.dot(x, pick.astype(F32), precision=HI, preferred_element_type=F32)


def well_cols(z, zl, zr, coef, diag, proc, target):
    cols = z.shape[1]
    return pl.pallas_call(
        cols_kernel,
        out_shape=(
            jax.ShapeDtypeStruct((HALF, cols), F32),
            jax.ShapeDtypeStruct((HALF, NGY), F32),
        ),
        in_specs=vmem(7),
        out_specs=tuple(vmem(2)),
        cost_estimate=cost(12 * HALF * cols * NGY, 4 * HALF * cols * 4),
        name="well_cols",
    )(z, zl, zr, coef, diag, proc, target)


def predict_kernel(start, p_ref, up_ref, dn_ref, el_ref, er_ref, rc_ref, cc_ref, proc_ref, o_ref):
    g = pl.program_id(0)
    last = pl.num_programs(0) - 1
    cols = p_ref.shape[1]
    tiles = cols // NGY
    here = pl.multiple_of(g * NGY, NGY)
    before = pl.multiple_of(jnp.maximum(g - 1, 0) * NGY, NGY)
    after = pl.multiple_of(jnp.minimum(g + 1, last) * NGY, NGY)
    wide = (NGY, NGY)
    rc = [jnp.broadcast_to(rc_ref[:, k : k + 1], wide) for k in range(5)]

    def left_tile(mid, above, below):
        total = rc[0] * mid + rc[1] * above + rc[2] * below
        return total + rc[3] * pltpu.roll(mid, 1, 0) + rc[4] * pltpu.roll(mid, NGY - 1, 0)

    parts = []
    for ref, t in [(el_ref, None)] + [(p_ref, t) for t in range(tiles)] + [(er_ref, None)]:
        if t is None:
            mid = ref[pl.ds(here + NGY, NGY), :]
            above = ref[pl.ds(here, NGY), :]
            below = ref[pl.ds(here + 2 * NGY, NGY), :]
        else:
            lanes = slice(t * NGY, (t + 1) * NGY)
            mid = p_ref[pl.ds(here, NGY), lanes]
            above = jnp.where(g == 0, up_ref[:, lanes], p_ref[pl.ds(before, NGY), lanes])
            below = jnp.where(g == last, dn_ref[:, lanes], p_ref[pl.ds(after, NGY), lanes])
        parts.append(left_tile(mid, above, below))
        if len(parts) >= 3:
            k = len(parts) - 3
            o_ref[:, k * NGY : (k + 1) * NGY] = across_lanes(parts, cc_ref[...], k, k + 1)[0]
    hit = start[0] + g
    eye = lax.broadcasted_iota(jnp.int32, wide, 0) == lax.broadcasted_iota(jnp.int32, wide, 1)
    for t in range(tiles):

        @pl.when(hit == t)
        def _():
            lanes = slice(t * NGY, (t + 1) * NGY)
            o_ref[:, lanes] = o_ref[:, lanes] + jnp.where(eye, proc_ref[:, lanes], 0.0)


def predict(start, block, up, dn, el, er, row_coef, col_coef, proc):
    rows, cols = block.shape
    steps = rows // NGY
    return pl.pallas_call(
        predict_kernel,
        out_shape=jax.ShapeDtypeStruct((rows, cols), F32),
        grid_spec=pltpu.PrefetchScalarGridSpec(
            num_scalar_prefetch=1,
            grid=(steps,),
            in_specs=vmem(5)
            + [pl.BlockSpec((NGY, 8), lambda g, s: (g, 0))]
            + vmem(2),
            out_specs=pl.BlockSpec((NGY, cols), lambda g, s: (g, 0)),
        ),
        compiler_params=pltpu.CompilerParams(vmem_limit_bytes=32 << 20),
        cost_estimate=cost(22 * rows * cols, 8 * rows * cols),
        name="predict",
    )(start, block, up, dn, el, er, row_coef, col_coef, proc)


BLK = 32


def small_inverse(d):
    size = d.shape[0]
    sub = lax.broadcasted_iota(jnp.int32, d.shape, 0)
    lane = lax.broadcasted_iota(jnp.int32, d.shape, 1)
    for j in range(size):
        row = d[j : j + 1, :]
        col = d[:, j : j + 1]
        inv = 1.0 / d[j : j + 1, j : j + 1]
        row = jnp.where(lane[0:1] == j, 1.0, row) * inv
        col = jnp.where(sub[:, 0:1] == j, -1.0, col)
        d = jnp.where((sub == j) | (lane == j), 0.0, d) - col * row
    return d


def dot(a, b):
    return jnp.dot(a, b, precision=HI, preferred_element_type=F32)


def inverse_kernel(own_ref, other_ref, rslot_ref, cslot_ref, noise_ref, o_ref, s_ref):
    rows_in = ROWS * HALF
    pick_rows = (lax.broadcasted_iota(jnp.int32, (M, rows_in), 1) == rslot_ref[...]).astype(F32)
    total = jnp.zeros((M, M), F32)
    for k, ref in enumerate((own_ref, other_ref)):
        for h in range(2):
            piece = ref[:, h].reshape(rows_in, NGY)
            some = dot(pick_rows, piece)
            base = (2 * k + h) * NGY
            pick = lax.broadcasted_iota(jnp.int32, (NGY, M), 0) + base == cslot_ref[...]
            total = total + dot(some, pick.astype(F32))
    i0 = lax.broadcasted_iota(jnp.int32, (M, M), 0)
    i1 = lax.broadcasted_iota(jnp.int32, (M, M), 1)
    s_ref[...] = total + jnp.where(i0 == i1, noise_ref[...], 0.0)
    sub = lax.broadcasted_iota(jnp.int32, (M, BLK), 0)
    for b in range(M // BLK):
        lo = b * BLK
        inv = small_inverse(s_ref[lo : lo + BLK, lo : lo + BLK])
        panel = s_ref[lo : lo + BLK, :]
        col = s_ref[:, lo : lo + BLK]
        here = (i1[0:BLK] >= lo) & (i1[0:BLK] < lo + BLK)
        scaled = dot(inv, panel)
        inside = (sub >= lo) & (sub < lo + BLK)
        upd = dot(jnp.where(inside, 0.0, col), scaled)
        down = dot(col, inv)
        s_ref[...] = s_ref[...] - upd
        s_ref[:, lo : lo + BLK] = -down
        s_ref[lo : lo + BLK, :] = scaled
        s_ref[lo : lo + BLK, lo : lo + BLK] = inv
    o_ref[...] = s_ref[...]


def inverse(own, other, rslot, cslot, noise):
    return pl.pallas_call(
        inverse_kernel,
        out_shape=jax.ShapeDtypeStruct((M, M), F32),
        in_specs=vmem(5),
        out_specs=vmem(1)[0],
        scratch_shapes=[pltpu.VMEM((M, M), F32)],
        compiler_params=pltpu.CompilerParams(vmem_limit_bytes=24 << 20),
        cost_estimate=cost(2 * 1153000000 * 8, 4 << 20),
        name="inverse",
    )(own, other, rslot, cslot, noise)


def split(x):
    high = x.astype(BF16)
    return high, (x - high.astype(F32)).astype(BF16)


def bdot(a, b, dims=((1,), (0,))):
    return lax.dot_general(a, b, (dims, ((), ())), preferred_element_type=F32)


def update_kernel(pred_ref, xc_ref, xr_ref, inv_ref, cslot_ref, rslot_ref, o_ref, uh, ul, sh, sl):
    j = pl.program_id(1)

    @pl.when((pl.program_id(0) == 0) & (j == 0))
    def _():
        pick = (lax.broadcasted_iota(jnp.int32, (M, SLOTS), 1) == cslot_ref[...]).astype(F32)
        across = dot(pick, xc_ref[...])
        high, low = split(dot(inv_ref[...], across))
        uh[...] = high
        ul[...] = low

    @pl.when(j == 0)
    def _():
        size = xr_ref.shape[-1]
        strip = xr_ref[...].reshape(SLOTS, size)
        pick = (lax.broadcasted_iota(jnp.int32, (SLOTS, M), 0) == rslot_ref[...]).astype(BF16)
        high, low = split(strip)
        sh[...] = bdot(high, pick, ((0,), (0,))).astype(BF16)
        sl[...] = bdot(low, pick, ((0,), (0,))).astype(BF16)

    size = o_ref.shape[0]
    rows = pl.ds(pl.multiple_of(j * size, size), size)
    a, b = sh[rows, :], sl[rows, :]
    o_ref[...] = pred_ref[...] - (bdot(a, uh[...]) + (bdot(a, ul[...]) + bdot(b, uh[...])))


def update(pred, xc, xr, inv, cslot, rslot):
    rows, cols = pred.shape
    tile = 256
    half = rows // 2
    steps = half // tile
    return pl.pallas_call(
        update_kernel,
        out_shape=jax.ShapeDtypeStruct((rows, cols), F32),
        grid=(2, steps),
        in_specs=[
            pl.BlockSpec((tile, cols), lambda k, j: (k * steps + j, 0)),
            pl.BlockSpec(memory_space=pltpu.VMEM),
            pl.BlockSpec((ROWS, None, HALF, half), lambda k, j: (0, k, 0, 0)),
        ]
        + vmem(3),
        out_specs=pl.BlockSpec((tile, cols), lambda k, j: (k * steps + j, 0)),
        scratch_shapes=[
            pltpu.VMEM((M, cols), BF16),
            pltpu.VMEM((M, cols), BF16),
            pltpu.VMEM((half, M), BF16),
            pltpu.VMEM((half, M), BF16),
        ],
        compiler_params=pltpu.CompilerParams(vmem_limit_bytes=40 << 20),
        cost_estimate=cost(6 * rows * cols * M, 8 * rows * cols),
        name="update",
    )(pred, xc, xr, inv, cslot, rslot)


def shift(x, axis, count, back):
    return lax.ppermute(x, axis, [((i + back) % count, i) for i in range(count)])


def flip(x, axis, count, bit):
    return lax.ppermute(x, axis, [(i, i ^ bit) for i in range(count)])


def shards(covariance, center, links, process, wells, noise):
    r = lax.axis_index("row")
    c = lax.axis_index("col")
    rows, cols = covariance.shape
    cells = center.shape[0]
    row_start, col_start = r * rows, c * cols
    block = covariance

    w = wells[0]
    part = w // cols
    slot_i = jnp.arange(M, dtype=jnp.int32)
    same = (part[:, None] == part[None, :]) & (slot_i[None, :] < slot_i[:, None])
    rank = jnp.sum(same.astype(jnp.int32), axis=1)
    slot = part * WMAX + rank
    hits = slot[None, :] == jnp.arange(SLOTS, dtype=jnp.int32)[:, None]
    slot_cell = jnp.max(jnp.where(hits, w[None, :], -1), axis=1)

    gy = jnp.arange(cells, dtype=jnp.int32) % NGY
    coef = jnp.concatenate(
        [
            center[None],
            links[0:2],
            jnp.where(gy == 0, 0.0, links[2])[None],
            jnp.where(gy == NGY - 1, 0.0, links[3])[None],
            process[None],
        ]
    )
    col_coef = lax.dynamic_slice_in_dim(coef, col_start, cols, 1)
    row_coef = jnp.concatenate(
        [lax.dynamic_slice_in_dim(coef, row_start, rows, 1), jnp.zeros((2, rows), F32)]
    ).T

    mine = lax.dynamic_slice_in_dim(slot_cell, r * HALF, HALF)
    valid = mine >= 0
    safe = jnp.maximum(mine, 0)
    at = jnp.take(coef, safe, axis=1)
    at = jnp.where(valid[None, :], at, 0.0)
    local = jnp.where(valid, mine - row_start, 0)
    first = local < NGY
    final = local >= rows - NGY
    five = jnp.stack([local, local - NGY, local + NGY, local - 1, local + 1])
    idx = jnp.clip(five, 0, rows - 1)
    inside = jnp.stack([valid, ~first, ~final, valid, valid])
    row_scale = jnp.where(inside, at[:5], 0.0)
    above = jnp.where(first, at[1], 0.0)[:, None]
    below = jnp.where(final, at[2], 0.0)[:, None]
    padded = jnp.concatenate([jnp.zeros((WMAX,), jnp.int32), slot_cell, jnp.zeros((WMAX,), jnp.int32)])
    next_cells = lax.dynamic_slice_in_dim(padded, (r + 1) * HALF + WMAX, WMAX)
    prev_cells = lax.dynamic_slice_in_dim(padded, r * HALF, WMAX)
    send = jnp.clip(
        jnp.stack([next_cells - NGY, prev_cells + NGY]) - row_start, 0, rows - 1
    )

    z, send_up, send_dn = well_rows(idx, row_scale, send, block)
    got_up = lax.ppermute(send_up, "row", [(i, i + 1) for i in range(ROWS - 1)])
    got_dn = lax.ppermute(send_dn, "row", [(i + 1, i) for i in range(ROWS - 1)])
    z = jnp.concatenate(
        [z[:WMAX] + above[:WMAX] * got_up, z[WMAX:] + below[WMAX:] * got_dn]
    )
    zl = lax.ppermute(z[:, cols - NGY :], "col", [(i, i + 1) for i in range(COLS - 1)])
    zr = lax.ppermute(z[:, :NGY], "col", [(i + 1, i) for i in range(COLS - 1)])
    here = lax.dynamic_slice_in_dim(slot_cell, c * WMAX, WMAX) - col_start
    lane = jnp.arange(NGY, dtype=jnp.int32)
    xq = c // 4
    target = jnp.where(lane // WMAX == xq, jnp.tile(here, NGY // WMAX), -1)[None]
    x, g = well_cols(
        z, zl, zr, col_coef[:5], (mine - col_start)[:, None], at[5][:, None], target
    )

    xc = lax.all_gather(x, "row", axis=0, tiled=True)
    turn = [
        (a * COLS + 2 * b + k, b * COLS + 2 * a + k)
        for a in range(ROWS)
        for b in range(ROWS)
        for k in range(2)
    ]
    turned = lax.ppermute(x, ("row", "col"), turn)
    xr = lax.all_gather(turned, "col", axis=0, tiled=False).reshape(ROWS, 2, HALF, cols)

    g = g + shift(g, "col", COLS, 4) + shift(g, "col", COLS, 8) + shift(g, "col", COLS, 12)
    g = jnp.stack([g, flip(g, "col", COLS, 2)])
    g = jnp.stack([g, flip(g, "row", ROWS, 1)])
    g = jnp.stack([g] + [shift(g, "row", ROWS, 2 * d) for d in range(1, 4)])
    g = g.reshape(ROWS, 2, HALF, NGY)
    g_other = flip(g, "col", COLS, 1)
    wr, wc = slot // HALF, slot // WMAX
    z_rel = (wr // 2 - r // 2) % 4
    row_slot = (z_rel * 2 + (wr % 2 ^ r % 2)) * HALF + slot % HALF
    col_slot = (
        (wc % 2 ^ c % 2) * (2 * NGY)
        + ((wc // 2) % 2 ^ (c // 2) % 2) * NGY
        + (wc // 4) * WMAX
        + slot % WMAX
    )
    inv = inverse(g, g_other, row_slot[:, None], col_slot[None], noise)

    up = lax.ppermute(block[rows - NGY :], "row", [(i, i + 1) for i in range(ROWS - 1)])
    dn = lax.ppermute(block[:NGY], "row", [(i + 1, i) for i in range(ROWS - 1)])
    right_edge = jnp.concatenate([a[:, cols - NGY :] for a in (up, block, dn)])
    left_edge = jnp.concatenate([a[:, :NGY] for a in (up, block, dn)])
    el = lax.ppermute(right_edge, "col", [(i, i + 1) for i in range(COLS - 1)])
    er = lax.ppermute(left_edge, "col", [(i + 1, i) for i in range(COLS - 1)])
    start = ((row_start - col_start) // NGY)[None]
    pred = predict(start, block, up, dn, el, er, row_coef, col_coef[:5], col_coef[5:6])

    return update(pred, xc, xr, inv, slot[:, None], slot[None])


def solution(mesh):
    in_specs = (P("row", "col"), P(), P(), P(), P(), P())
    out_specs = P("row", "col")
    return jax.shard_map(shards, mesh=mesh, in_specs=in_specs, out_specs=out_specs, check_vma=False)
```

```python
import functools

import jax
import jax.numpy as jnp
from jax import lax
from jax.experimental import pallas as pl
from jax.experimental.pallas import tpu as pltpu
from jax.sharding import PartitionSpec as P

NGY = 128
M = 256
WMAX = 32
ROWS = 8
COLS = 16
HALF = 2 * WMAX
SLOTS = ROWS * HALF
F32 = jnp.float32
BF16 = jnp.bfloat16
HI = lax.Precision.HIGHEST


def cost(flops, size):
    return pl.CostEstimate(flops=flops, bytes_accessed=size, transcendentals=0)


def vmem(count):
    return [pl.BlockSpec(memory_space=pltpu.VMEM)] * count


def rows_kernel(
    place, wells, center, links, process, block,
    z_ref, dn_ref, aux_ref, target_ref, local_ref,
    p_ref, own, side, noise, cell, count, sems,
):
    rows, cols = p_ref.shape
    r, c = place[0], place[1]
    row_start, col_start = pl.multiple_of(r * rows, rows), c * cols
    part = pl.ds(row_start, rows)
    copies = [
        pltpu.make_async_copy(block, p_ref, sems.at[0]),
        pltpu.make_async_copy(center.at[part], own, sems.at[1]),
        pltpu.make_async_copy(links.at[:, part], side, sems.at[2]),
        pltpu.make_async_copy(process.at[part], noise, sems.at[3]),
    ]
    for copy in copies:
        copy.start()

    for i in range(SLOTS // WMAX):
        count[i] = 0

    def none(i, carry):
        for k in range(16):
            cell[i * 16 + k] = -1
        return carry

    lax.fori_loop(0, SLOTS // 16, none, 0)

    def put(m, carry):
        w = wells[0, m]
        home = w // cols
        n = count[home]
        cell[home * WMAX + n] = w
        count[home] = n + 1
        return carry

    lax.fori_loop(0, M, put, 0, unroll=8)
    for copy in copies:
        copy.wait()

    lane = lax.broadcasted_iota(jnp.int32, (1, NGY), 1)
    top = ROWS - 1

    def one(s, carry):
        w = cell[r * HALF + s]
        good = w >= 0
        i = jnp.where(good, w - row_start, 0)
        first, final = i < NGY, i >= rows - NGY
        gy = i % NGY
        gate = jnp.where(good, 1.0, 0.0)
        k0, k1, k2 = own[i] * gate, side[0, i] * gate, side[1, i] * gate
        k3 = jnp.where(gy == 0, 0.0, side[2, i] * gate)
        k4 = jnp.where(gy == NGY - 1, 0.0, side[3, i] * gate)
        total = k0 * p_ref[pl.ds(i, 1), :]
        above = p_ref[pl.ds(jnp.maximum(i - NGY, 0), 1), :]
        below = p_ref[pl.ds(jnp.minimum(i + NGY, rows - 1), 1), :]
        total = total + jnp.where(first, 0.0, k1) * above + jnp.where(final, 0.0, k2) * below
        before = p_ref[pl.ds(jnp.maximum(i - 1, 0), 1), :]
        after = p_ref[pl.ds(jnp.minimum(i + 1, rows - 1), 1), :]
        z_ref[pl.ds(s, 1), :] = total + k3 * before + k4 * after
        row = jnp.where(lane == 0, jnp.where(first & (r > 0), k1, 0.0), 0.0)
        row = jnp.where(lane == 1, jnp.where(final & (r < top), k2, 0.0), row)
        row = jnp.where(lane == 2, noise[i] * gate, row)
        col = jnp.where(good, w - col_start, -1)
        row = jnp.where(lane == 3, jnp.full((1, NGY), col, jnp.int32).astype(F32), row)
        aux_ref[pl.ds(s, 1), :] = row
        return carry

    lax.fori_loop(0, HALF, one, 0, unroll=4)

    def two(s, carry):
        dn = cell[jnp.maximum(r * HALF - WMAX + s, 0)] + NGY - row_start
        dn_ref[pl.ds(s, 1), :] = p_ref[pl.ds(jnp.clip(dn, 0, rows - 1), 1), :]
        local_ref[s] = jnp.clip(cell[r * HALF + s] - row_start, 0, NGY - 1)
        return carry

    lax.fori_loop(0, WMAX, two, 0, unroll=4)

    base = (c // 4) * WMAX

    def three(t, row):
        return jnp.where(lane == base + t, cell[c * WMAX + t] - col_start, row)

    target_ref[...] = lax.fori_loop(0, WMAX, three, jnp.full((1, NGY), -1, jnp.int32), unroll=4)


def well_rows(place, wells, center, links, process, block):
    rows, cols = block.shape
    smem = pl.BlockSpec(memory_space=pltpu.SMEM)
    hbm = pl.BlockSpec(memory_space=pltpu.HBM)
    return pl.pallas_call(
        rows_kernel,
        out_shape=(
            jax.ShapeDtypeStruct((HALF, cols), F32),
            jax.ShapeDtypeStruct((WMAX, cols), F32),
            jax.ShapeDtypeStruct((HALF, NGY), F32),
            jax.ShapeDtypeStruct((1, NGY), jnp.int32),
            jax.ShapeDtypeStruct((WMAX,), jnp.int32),
        ),
        in_specs=[smem, smem, hbm, hbm, hbm, hbm],
        out_specs=tuple(vmem(4)) + (smem,),
        scratch_shapes=[
            pltpu.VMEM((rows, cols), F32),
            pltpu.SMEM((rows,), F32),
            pltpu.SMEM((4, rows), F32),
            pltpu.SMEM((rows,), F32),
            pltpu.SMEM((SLOTS,), jnp.int32),
            pltpu.SMEM((SLOTS // WMAX,), jnp.int32),
            pltpu.SemaphoreType.DMA((4,)),
        ],
        compiler_params=pltpu.CompilerParams(vmem_limit_bytes=24 << 20),
        cost_estimate=cost(10 * HALF * cols, block.size * 4),
        name="well_rows",
    )(place, wells, center, links, process, block)


def merge_kernel(local, z_ref, aux_ref, up_ref, dn_ref, o_ref, left_ref, right_ref):
    cols = z_ref.shape[1]
    scale = aux_ref[...]

    def one(s, carry):
        o_ref[pl.ds(s, 1), :] = up_ref[pl.ds(local[s], 1), :]
        return carry

    lax.fori_loop(0, WMAX, one, 0, unroll=4)
    o_ref[0:WMAX] = z_ref[0:WMAX] + scale[0:WMAX, 0:1] * o_ref[0:WMAX]
    o_ref[WMAX:] = z_ref[WMAX:] + scale[WMAX:, 1:2] * dn_ref[...]
    left_ref[...] = o_ref[:, 0:NGY]
    right_ref[...] = o_ref[:, cols - NGY :]


def merge(local, z, aux, up, dn):
    cols = z.shape[1]
    return pl.pallas_call(
        merge_kernel,
        out_shape=(
            jax.ShapeDtypeStruct((HALF, cols), F32),
            jax.ShapeDtypeStruct((HALF, NGY), F32),
            jax.ShapeDtypeStruct((HALF, NGY), F32),
        ),
        in_specs=[pl.BlockSpec(memory_space=pltpu.SMEM)] + vmem(4),
        out_specs=tuple(vmem(3)),
        cost_estimate=cost(4 * HALF * cols, 4 * HALF * cols * 4),
        name="merge",
    )(local, z, aux, up, dn)


def across_lanes(parts, coef, lo, hi):
    out = []
    for t in range(lo, hi):
        left, mid, right = parts[t], parts[t + 1], parts[t + 2]
        c = coef[:, t * NGY : (t + 1) * NGY]
        total = c[0:1] * mid
        if left is not None:
            total = total + c[1:2] * left
        if right is not None:
            total = total + c[2:3] * right
        total = total + c[3:4] * pltpu.roll(mid, 1, 1) + c[4:5] * pltpu.roll(mid, NGY - 1, 1)
        out.append(total)
    return out


def cols_kernel(z_ref, zl_ref, zr_ref, coef_ref, aux_ref, target_ref, x_ref, g_ref):
    cols = z_ref.shape[1]
    tiles = cols // NGY
    parts = [zl_ref[...]] + [z_ref[:, t * NGY : (t + 1) * NGY] for t in range(tiles)] + [zr_ref[...]]
    out = across_lanes(parts, coef_ref[...], 0, tiles)
    x = jnp.concatenate(out, axis=1)
    lane = lax.broadcasted_iota(jnp.int32, x.shape, 1)
    x = x + jnp.where(lane.astype(F32) == aux_ref[:, 3:4], aux_ref[:, 2:3], 0.0)
    x_ref[...] = x
    pick = lax.broadcasted_iota(jnp.int32, (cols, NGY), 0) == target_ref[...]
    g_ref[...] = jnp.dot(x, pick.astype(F32), precision=HI, preferred_element_type=F32)


def well_cols(z, zl, zr, coef, aux, target):
    cols = z.shape[1]
    return pl.pallas_call(
        cols_kernel,
        out_shape=(
            jax.ShapeDtypeStruct((HALF, cols), F32),
            jax.ShapeDtypeStruct((HALF, NGY), F32),
        ),
        in_specs=vmem(6),
        out_specs=tuple(vmem(2)),
        cost_estimate=cost(12 * HALF * cols * NGY, 4 * HALF * cols * 4),
        name="well_cols",
    )(z, zl, zr, coef, aux, target)


def left_tile(rc, mid, above, below):
    total = rc[0] * mid + rc[1] * above + rc[2] * below
    return total + rc[3] * pltpu.roll(mid, 1, 0) + rc[4] * pltpu.roll(mid, NGY - 1, 0)


def predict_kernel(start, p_ref, rc_ref, cc_ref, proc_ref, o_ref):
    g = pl.program_id(0)
    last = pl.num_programs(0) - 1
    cols = p_ref.shape[1]
    tiles = cols // NGY
    here = pl.ds(pl.multiple_of(g * NGY, NGY), NGY)
    before = pl.ds(pl.multiple_of(jnp.maximum(g - 1, 0) * NGY, NGY), NGY)
    after = pl.ds(pl.multiple_of(jnp.minimum(g + 1, last) * NGY, NGY), NGY)
    wide = (NGY, NGY)
    rc = [jnp.broadcast_to(rc_ref[:, k : k + 1], wide) for k in range(5)]
    rc[1] = jnp.where(g == 0, 0.0, rc[1])
    rc[2] = jnp.where(g == last, 0.0, rc[2])
    parts = [None]
    for t in range(tiles + 1):
        if t < tiles:
            lanes = slice(t * NGY, (t + 1) * NGY)
            parts.append(left_tile(rc, p_ref[here, lanes], p_ref[before, lanes], p_ref[after, lanes]))
        else:
            parts.append(None)
        if t >= 1:
            o_ref[:, (t - 1) * NGY : t * NGY] = across_lanes(parts, cc_ref[...], t - 1, t)[0]
    hit = start[0] + g
    eye = lax.broadcasted_iota(jnp.int32, wide, 0) == lax.broadcasted_iota(jnp.int32, wide, 1)
    for t in range(tiles):

        @pl.when(hit == t)
        def _():
            lanes = slice(t * NGY, (t + 1) * NGY)
            o_ref[:, lanes] = o_ref[:, lanes] + jnp.where(eye, proc_ref[:, lanes], 0.0)


def predict(start, block, row_coef, col_coef, proc):
    rows, cols = block.shape
    steps = rows // NGY
    return pl.pallas_call(
        predict_kernel,
        out_shape=jax.ShapeDtypeStruct((rows, cols), F32),
        grid_spec=pltpu.PrefetchScalarGridSpec(
            num_scalar_prefetch=1,
            grid=(steps,),
            in_specs=vmem(1) + [pl.BlockSpec((NGY, 8), lambda g, s: (g, 0))] + vmem(2),
            out_specs=pl.BlockSpec((NGY, cols), lambda g, s: (g, 0)),
        ),
        compiler_params=pltpu.CompilerParams(vmem_limit_bytes=24 << 20),
        cost_estimate=cost(22 * rows * cols, 8 * rows * cols),
        name="predict",
    )(start, block, row_coef, col_coef, proc)


BLK = 128
STEP = 4


def inverse_two(a, b, c):
    q = 1.0 / (a * c - b * b)
    return c * q, -b * q, a * q


def inverse_four(e):
    a, b, c = inverse_two(e[0][0], e[0][1], e[1][1])
    two = range(2)
    side = [[e[i][2 + k] for k in two] for i in two]
    w = [
        [a * side[0][k] + b * side[1][k] for k in two],
        [b * side[0][k] + c * side[1][k] for k in two],
    ]
    s = [
        [e[2 + i][2 + k] - (side[0][i] * w[0][k] + side[1][i] * w[1][k]) for k in two] for i in two
    ]
    p, q, t = inverse_two(s[0][0], s[0][1], s[1][1])
    v = [[w[i][0] * p + w[i][1] * q, w[i][0] * q + w[i][1] * t] for i in two]
    t00 = a + v[0][0] * w[0][0] + v[0][1] * w[0][1]
    t01 = b + v[0][0] * w[1][0] + v[0][1] * w[1][1]
    t11 = c + v[1][0] * w[1][0] + v[1][1] * w[1][1]
    return [
        [t00, t01, -v[0][0], -v[0][1]],
        [t01, t11, -v[1][0], -v[1][1]],
        [-v[0][0], -v[1][0], p, q],
        [-v[0][1], -v[1][1], q, t],
    ]


def small_inverse(d):
    size = d.shape[0]
    wide = (8, size)
    chunks = [d[8 * q : 8 * q + 8] for q in range(size // 8)]
    sub = lax.broadcasted_iota(jnp.int32, wide, 0)
    lane = lax.broadcasted_iota(jnp.int32, wide, 1)
    four = range(STEP)
    for j in range(0, size, STEP):
        home, o = divmod(j, 8)
        row = [jnp.broadcast_to(chunks[home][o + a : o + a + 1], wide) for a in four]
        e = [[None] * STEP for _ in four]
        for a in four:
            for b in range(a, STEP):
                e[a][b] = e[b][a] = jnp.broadcast_to(row[a][:, j + b : j + b + 1], wide)
        piv = inverse_four(e)
        inside = (lane >= j) & (lane < j + STEP)
        row = [jnp.where(lane == j + a, 1.0, jnp.where(inside, 0.0, row[a])) for a in four]
        new = [
            (piv[a][0] * row[0] + piv[a][1] * row[1]) + (piv[a][2] * row[2] + piv[a][3] * row[3])
            for a in four
        ]
        out = []
        for q, chunk in enumerate(chunks):
            col = [jnp.broadcast_to(chunk[:, j + a : j + a + 1], wide) for a in four]
            less = (col[0] * new[0] + col[1] * new[1]) + (col[2] * new[2] + col[3] * new[3])
            rest = jnp.where(inside, 0.0, chunk) - less
            if q == home:
                for a in four:
                    rest = jnp.where(sub == o + a, new[a], rest)
            out.append(rest)
        chunks = out
    return jnp.concatenate(chunks, axis=0)


def dot(a, b):
    return jnp.dot(a, b, precision=HI, preferred_element_type=F32)


def inverse_kernel(own_ref, other_ref, rslot_ref, cslot_ref, noise_ref, o_ref, s_ref):
    rows_in = ROWS * HALF
    pick_rows = (lax.broadcasted_iota(jnp.int32, (M, rows_in), 1) == rslot_ref[...]).astype(F32)
    total = jnp.zeros((M, M), F32)
    for k, ref in enumerate((own_ref, other_ref)):
        for h in range(2):
            piece = ref[:, h].reshape(rows_in, NGY)
            some = dot(pick_rows, piece)
            base = (2 * k + h) * NGY
            pick = lax.broadcasted_iota(jnp.int32, (NGY, M), 0) + base == cslot_ref[...]
            total = total + dot(some, pick.astype(F32))
    i0 = lax.broadcasted_iota(jnp.int32, (M, M), 0)
    i1 = lax.broadcasted_iota(jnp.int32, (M, M), 1)
    s_ref[...] = total + jnp.where(i0 == i1, noise_ref[...], 0.0)
    sub = lax.broadcasted_iota(jnp.int32, (M, BLK), 0)
    for b in range(M // BLK):
        lo = b * BLK
        inv = small_inverse(s_ref[lo : lo + BLK, lo : lo + BLK])
        panel = s_ref[lo : lo + BLK, :]
        col = s_ref[:, lo : lo + BLK]
        here = (i1[0:BLK] >= lo) & (i1[0:BLK] < lo + BLK)
        scaled = dot(inv, panel)
        inside = (sub >= lo) & (sub < lo + BLK)
        upd = dot(jnp.where(inside, 0.0, col), scaled)
        down = dot(col, inv)
        s_ref[...] = s_ref[...] - upd
        s_ref[:, lo : lo + BLK] = -down
        s_ref[lo : lo + BLK, :] = scaled
        s_ref[lo : lo + BLK, lo : lo + BLK] = inv
    o_ref[...] = s_ref[...]


def inverse(own, other, rslot, cslot, noise):
    return pl.pallas_call(
        inverse_kernel,
        out_shape=jax.ShapeDtypeStruct((M, M), F32),
        in_specs=vmem(5),
        out_specs=vmem(1)[0],
        scratch_shapes=[pltpu.VMEM((M, M), F32)],
        compiler_params=pltpu.CompilerParams(vmem_limit_bytes=24 << 20),
        cost_estimate=cost(2 * 1153000000 * 8, 4 << 20),
        name="inverse",
    )(own, other, rslot, cslot, noise)


def split(x):
    high = x.astype(BF16)
    return high, (x - high.astype(F32)).astype(BF16)


def bdot(a, b, dims=((1,), (0,))):
    return lax.dot_general(a, b, (dims, ((), ())), preferred_element_type=F32)


def three(x):
    high, low = split(x)
    return high, low, (x - high.astype(F32) - low.astype(F32)).astype(BF16)


def joined(refs):
    return jnp.concatenate([p[...].reshape(-1, p.shape[-1]) for p in refs], axis=0)


def across_kernel(slot_ref, *refs):
    pick = (lax.broadcasted_iota(jnp.int32, (M, SLOTS), 1) == slot_ref[...]).astype(BF16)
    high, mid, low = three(joined(refs[:-1]))
    refs[-1][...] = bdot(pick, high) + (bdot(pick, mid) + bdot(pick, low))


def across(slot, parts):
    cols = parts[0].shape[-1]
    return pl.pallas_call(
        across_kernel,
        out_shape=jax.ShapeDtypeStruct((M, cols), F32),
        in_specs=vmem(1 + len(parts)),
        out_specs=vmem(1)[0],
        compiler_params=pltpu.CompilerParams(vmem_limit_bytes=24 << 20),
        cost_estimate=cost(6 * M * SLOTS * cols, 3 * SLOTS * cols * 4),
        name="across",
    )(slot, *parts)


def strip_kernel(slot_ref, *refs):
    pick = (lax.broadcasted_iota(jnp.int32, (SLOTS, M), 0) == slot_ref[...]).astype(BF16)
    high, low = split(joined(refs[:-2]))
    refs[-2][...] = bdot(high, pick, ((0,), (0,))).astype(BF16)
    refs[-1][...] = bdot(low, pick, ((0,), (0,))).astype(BF16)


def strip(slot, parts):
    size = parts[0].shape[-1]
    return pl.pallas_call(
        strip_kernel,
        out_shape=(jax.ShapeDtypeStruct((size, M), BF16), jax.ShapeDtypeStruct((size, M), BF16)),
        in_specs=vmem(1 + len(parts)),
        out_specs=tuple(vmem(2)),
        compiler_params=pltpu.CompilerParams(vmem_limit_bytes=24 << 20),
        cost_estimate=cost(4 * M * SLOTS * size, 2 * SLOTS * size * 4),
        name="strip",
    )(slot, *parts)


def update_kernel(
    core, pred_ref, inv_ref, xc_ref, rc_ref, cc_ref, up_ref, dn_ref, el_ref, er_ref,
    oh_ref, ol_ref, ph_ref, pl_ref, o_ref, uh, ul,
):
    h, j = pl.program_id(0), pl.program_id(1)
    steps = pl.num_programs(1)
    g = (h ^ core[0]) * steps + j
    last = 2 * steps - 1

    @pl.when((h == 0) & (j == 0))
    def _():
        high, low = split(dot(inv_ref[...], xc_ref[...]))
        uh[...] = high
        ul[...] = low

    size, cols = o_ref.shape
    rows = pl.ds(pl.multiple_of(j * size, size), size)
    for half, (hi_ref, lo_ref) in enumerate(((oh_ref, ol_ref), (ph_ref, pl_ref))):

        @pl.when(h == half)
        def _():
            a, b = hi_ref[rows, :], lo_ref[rows, :]
            o_ref[...] = pred_ref[...] - (bdot(a, uh[...]) + (bdot(a, ul[...]) + bdot(b, uh[...])))

    rc = [jnp.broadcast_to(rc_ref[:, k : k + 1], (NGY, NGY)) for k in range(5)]
    above = pl.ds(pl.multiple_of(g * NGY, NGY), NGY)
    here = pl.ds(pl.multiple_of(g * NGY + NGY, NGY), NGY)
    below = pl.ds(pl.multiple_of(g * NGY + 2 * NGY, NGY), NGY)
    for ref, lo, k in ((el_ref, 0, 1), (er_ref, cols - NGY, 2)):
        rim = left_tile(rc, ref[here, :], ref[above, :], ref[below, :])
        lanes = slice(lo, lo + NGY)
        o_ref[:, lanes] = o_ref[:, lanes] + cc_ref[k : k + 1, lanes] * rim
    for at, ref, k in ((0, up_ref, 1), (last, dn_ref, 2)):

        @pl.when(g == at)
        def _():
            tiles = cols // NGY
            parts = [None] + [rc[k] * ref[:, t * NGY : (t + 1) * NGY] for t in range(tiles)] + [None]
            rim = across_lanes(parts, cc_ref[...], 0, tiles)
            o_ref[...] = o_ref[...] + jnp.concatenate(rim, axis=1)


def update(core, pred, inv, xc, row_coef, col_coef, rims, own, other):
    rows, cols = pred.shape
    half = rows // 2
    steps = half // NGY
    tile = pl.BlockSpec((NGY, cols), lambda h, j, k: ((h ^ k[0]) * steps + j, 0))
    few = pl.BlockSpec((NGY, 8), lambda h, j, k: ((h ^ k[0]) * steps + j, 0))
    return pl.pallas_call(
        update_kernel,
        out_shape=jax.ShapeDtypeStruct((rows, cols), F32),
        grid_spec=pltpu.PrefetchScalarGridSpec(
            num_scalar_prefetch=1,
            grid=(2, steps),
            in_specs=[tile] + vmem(2) + [few] + vmem(9),
            out_specs=tile,
            scratch_shapes=[pltpu.VMEM((M, cols), BF16), pltpu.VMEM((M, cols), BF16)],
        ),
        compiler_params=pltpu.CompilerParams(vmem_limit_bytes=32 << 20),
        cost_estimate=cost(6 * rows * cols * M, 8 * rows * cols),
        name="update",
    )(core, pred, inv, xc, row_coef, col_coef, *rims, *own, *other)


def shift(x, axis, count, back):
    return lax.ppermute(x, axis, [((i + back) % count, i) for i in range(count)])


def flip(x, axis, count, bit):
    return lax.ppermute(x, axis, [(i, i ^ bit) for i in range(count)])


def ring(x, axis, count, near, step):
    pair = jnp.stack([x, flip(x, axis, count, near)])
    more = shift(pair, axis, count, step)
    less = shift(pair, axis, count, count - step)
    far = shift(more[0], axis, count, step), shift(less[1], axis, count, count - step)
    return pair, more, far, less


def after(x, *others):
    return lax.optimization_barrier((x,) + others)[0]


def shards(covariance, center, links, process, wells, noise):
    r = lax.axis_index("row")
    c = lax.axis_index("col")
    rows, cols = covariance.shape
    cells = center.shape[0]
    row_start, col_start = r * rows, c * cols
    block = covariance

    up = shift(block[rows - NGY :], "row", ROWS, ROWS - 1)
    z, send_dn, aux, target, local = well_rows(
        jnp.stack([r, c]), wells, center, links, process, block
    )
    got_dn = shift(send_dn, "row", ROWS, 1)
    z, left, right = merge(local, z, aux, up, got_dn)
    zl = shift(right, "col", COLS, COLS - 1)
    zr = shift(left, "col", COLS, 1)

    cell = jnp.arange(cells, dtype=jnp.int32)
    gx, gy = cell // NGY, cell % NGY
    coef = jnp.concatenate(
        [
            center[None],
            jnp.where(gx == 0, 0.0, links[0])[None],
            jnp.where(gx == cells // NGY - 1, 0.0, links[1])[None],
            jnp.where(gy == 0, 0.0, links[2])[None],
            jnp.where(gy == NGY - 1, 0.0, links[3])[None],
            process[None],
        ]
    )
    coef = after(coef, send_dn)
    col_coef = lax.dynamic_slice_in_dim(coef, col_start, cols, 1)
    row_part = lax.dynamic_slice_in_dim(coef, row_start, rows, 1)
    x, g = well_cols(z, zl, zr, col_coef[:5], aux, target)

    g = g + shift(g, "col", COLS, 4) + shift(g, "col", COLS, 8) + shift(g, "col", COLS, 12)
    g = jnp.stack([g, flip(g, "col", COLS, 2)])
    g = jnp.stack([g, flip(g, "row", ROWS, 1)])
    g = jnp.stack([g] + [shift(g, "row", ROWS, 2 * d) for d in range(1, 4)])
    g = g.reshape(ROWS, 2, HALF, NGY)
    g_other = flip(g, "col", COLS, 1)

    turn = [
        (a * COLS + 2 * b + k, b * COLS + 2 * a + k)
        for a in range(ROWS)
        for b in range(ROWS)
        for k in range(2)
    ]
    turned = lax.ppermute(x, ("row", "col"), turn)
    pair, more, far, less = ring(x, "row", ROWS, 1, 2)
    x_parts = [pair, more, *far, less]
    pair, more, far, less = ring(turned, "col", COLS, 2, 4)
    own = [pair, more, *far, less]
    far = jnp.stack(far)
    other = [flip(a, "col", COLS, 1) for a in (pair, more, far, less)]

    dn = shift(after(block[:NGY], x), "row", ROWS, 1)
    right = jnp.concatenate([a[:, cols - NGY :] for a in (up, block, dn)])
    left = jnp.concatenate([a[:, :NGY] for a in (up, block, dn)])
    el = shift(after(right, turned), "col", COLS, COLS - 1)
    er = shift(after(left, turned), "col", COLS, 1)

    start = ((row_start - col_start) // NGY)[None]
    row_coef = jnp.concatenate([after(row_part, x), jnp.zeros((2, rows), F32)]).T
    pred = predict(start, block, row_coef, col_coef[:5], col_coef[5:6])

    w = after(wells, z)[0]
    part = w // cols
    number = jnp.arange(M, dtype=jnp.int32)
    same = (part[:, None] == part[None, :]) & (number[None, :] < number[:, None])
    rank = jnp.sum(same.astype(jnp.int32), axis=1)
    wr, wc = part // 2, part
    in_row = (wc % 2) * WMAX + rank
    row_slot = ((wr // 2 - r // 2) % 4 * 2 + (wr % 2 ^ r % 2)) * HALF + in_row
    strip_slot = ((wr // 2 - c // 4) % 4 * 2 + (wr % 2 ^ (c // 2) % 2)) * HALF + in_row
    col_slot = (
        (wc % 2 ^ c % 2) * (2 * NGY)
        + ((wc // 2) % 2 ^ (c // 2) % 2) * NGY
        + (wc // 4) * WMAX
        + rank
    )
    xc = across(row_slot[:, None], x_parts)
    own = strip(strip_slot[None], own)
    other = strip(strip_slot[None], other)
    inv = inverse(g, g_other, row_slot[:, None], col_slot[None], noise)
    rims = (up, dn, el, er)
    return update((c % 2)[None], pred, inv, xc, row_coef, col_coef[:5], rims, own, other)


def solution(mesh):
    in_specs = (P("row", "col"), P(), P(), P(), P(), P())
    out_specs = P("row", "col")
    return jax.shard_map(shards, mesh=mesh, in_specs=in_specs, out_specs=out_specs, check_vma=False)
```

```python
import functools

import jax
import jax.numpy as jnp
from jax import lax
from jax.experimental import pallas as pl
from jax.experimental.pallas import tpu as pltpu
from jax.sharding import PartitionSpec as P

NGY = 128
M = 256
WMAX = 32
ROWS = 8
COLS = 16
HALF = 2 * WMAX
SLOTS = ROWS * HALF
F32 = jnp.float32
BF16 = jnp.bfloat16
HI = lax.Precision.HIGHEST


def cost(flops, size):
    return pl.CostEstimate(flops=flops, bytes_accessed=size, transcendentals=0)


def vmem(count):
    return [pl.BlockSpec(memory_space=pltpu.VMEM)] * count


def table_kernel(
    place, wells, center, links, process, block,
    z_ref, up_ref, dn_ref, aux_ref, target_ref, top_ref, low_ref, left_ref, right_ref,
    p_ref, own, side, noise, cell, count, sems,
):
    rows, cols = block.shape
    r, c = place[0], place[1]
    row_start, col_start = pl.multiple_of(r * rows, rows), c * cols
    part = pl.ds(row_start, rows)
    copies = [
        pltpu.make_async_copy(block.at[pl.ds(0, NGY)], top_ref, sems.at[0]),
        pltpu.make_async_copy(block.at[pl.ds(rows - NGY, NGY)], low_ref, sems.at[1]),
        pltpu.make_async_copy(center.at[part], own, sems.at[2]),
        pltpu.make_async_copy(links.at[:, part], side, sems.at[3]),
        pltpu.make_async_copy(process.at[part], noise, sems.at[4]),
        pltpu.make_async_copy(block, p_ref, sems.at[5]),
    ]
    for copy in copies:
        copy.start()

    for i in range(SLOTS // WMAX):
        count[i] = 0

    def none(i, carry):
        for k in range(16):
            cell[i * 16 + k] = -1
        return carry

    lax.fori_loop(0, SLOTS // 16, none, 0)
    shift_by = cols.bit_length() - 1

    def put(m, carry):
        w = wells[0, m]
        home = w >> shift_by
        n = count[home]
        cell[home * WMAX + n] = w
        count[home] = n + 1
        return carry

    lax.fori_loop(0, M, put, 0, unroll=16)
    for copy in copies:
        copy.wait()

    left_ref[NGY : rows + NGY, :] = p_ref[:, 0:NGY]
    right_ref[NGY : rows + NGY, :] = p_ref[:, cols - NGY :]
    lane = lax.broadcasted_iota(jnp.int32, (1, NGY), 1)

    def two(s, carry):
        up = cell[jnp.minimum((r + 1) * HALF + s, SLOTS - 1)] - NGY - row_start - (rows - NGY)
        dn = cell[jnp.maximum(r * HALF - WMAX + s, 0)] + NGY - row_start
        up_ref[pl.ds(s, 1), :] = low_ref[pl.ds(jnp.clip(up, 0, NGY - 1), 1), :]
        dn_ref[pl.ds(s, 1), :] = top_ref[pl.ds(jnp.clip(dn, 0, NGY - 1), 1), :]
        return carry

    lax.fori_loop(0, WMAX, two, 0, unroll=4)

    def one(s, carry):
        w = cell[r * HALF + s]
        good = w >= 0
        i = jnp.where(good, w - row_start, 0)
        first, final = i < NGY, i >= rows - NGY
        gy = i & (NGY - 1)
        gate = jnp.where(good, 1.0, 0.0)
        k1, k2 = side[0, i] * gate, side[1, i] * gate
        k3 = jnp.where(gy == 0, 0.0, side[2, i] * gate)
        k4 = jnp.where(gy == NGY - 1, 0.0, side[3, i] * gate)
        low, high = jnp.maximum(i - 1, 0), jnp.minimum(i + 1, rows - 1)
        above, below = jnp.maximum(i - NGY, 0), jnp.minimum(i + NGY, rows - 1)
        total = (own[i] * gate) * p_ref[pl.ds(i, 1), :]
        total = total + jnp.where(first, 0.0, k1) * p_ref[pl.ds(above, 1), :]
        total = total + jnp.where(final, 0.0, k2) * p_ref[pl.ds(below, 1), :]
        z_ref[pl.ds(s, 1), :] = total + k3 * p_ref[pl.ds(low, 1), :] + k4 * p_ref[pl.ds(high, 1), :]
        row = jnp.where(lane == 0, jnp.where(first & (r > 0), k1, 0.0), 0.0)
        row = jnp.where(lane == 1, jnp.where(final & (r < ROWS - 1), k2, 0.0), row)
        row = jnp.where(lane == 2, noise[i] * gate, row)
        col = jnp.where(good, w - col_start, -1)
        row = jnp.where(lane == 3, jnp.full((1, NGY), col, jnp.int32).astype(F32), row)
        aux_ref[pl.ds(s, 1), :] = row
        return carry

    lax.fori_loop(0, HALF, one, 0, unroll=4)
    base = (c // 4) * WMAX

    def three(t, row):
        return jnp.where(lane == base + t, cell[c * WMAX + t] - col_start, row)

    target_ref[...] = lax.fori_loop(0, WMAX, three, jnp.full((1, NGY), -1, jnp.int32), unroll=4)


def tables(place, wells, center, links, process, block):
    rows, cols = block.shape
    smem = pl.BlockSpec(memory_space=pltpu.SMEM)
    hbm = pl.BlockSpec(memory_space=pltpu.HBM)
    return pl.pallas_call(
        table_kernel,
        out_shape=(
            jax.ShapeDtypeStruct((HALF, cols), F32),
            jax.ShapeDtypeStruct((WMAX, cols), F32),
            jax.ShapeDtypeStruct((WMAX, cols), F32),
            jax.ShapeDtypeStruct((HALF, NGY), F32),
            jax.ShapeDtypeStruct((1, NGY), jnp.int32),
            jax.ShapeDtypeStruct((NGY, cols), F32),
            jax.ShapeDtypeStruct((NGY, cols), F32),
            jax.ShapeDtypeStruct((rows + 2 * NGY, NGY), F32),
            jax.ShapeDtypeStruct((rows + 2 * NGY, NGY), F32),
        ),
        in_specs=[smem, smem, hbm, hbm, hbm, hbm],
        out_specs=tuple(vmem(9)),
        scratch_shapes=[
            pltpu.VMEM((rows, cols), F32),
            pltpu.SMEM((rows,), F32),
            pltpu.SMEM((4, rows), F32),
            pltpu.SMEM((rows,), F32),
            pltpu.SMEM((SLOTS,), jnp.int32),
            pltpu.SMEM((SLOTS // WMAX,), jnp.int32),
            pltpu.SemaphoreType.DMA((6,)),
        ],
        compiler_params=pltpu.CompilerParams(vmem_limit_bytes=60 << 20),
        cost_estimate=cost(1 << 20, 2 << 20),
        name="tables",
    )(place, wells, center, links, process, block)


def merge_kernel(z_ref, aux_ref, up_ref, dn_ref, o_ref, left_ref, right_ref):
    cols = z_ref.shape[1]
    scale = aux_ref[...]
    o_ref[0:WMAX] = z_ref[0:WMAX] + scale[0:WMAX, 0:1] * up_ref[...]
    o_ref[WMAX:] = z_ref[WMAX:] + scale[WMAX:, 1:2] * dn_ref[...]
    left_ref[...] = o_ref[:, 0:NGY]
    right_ref[...] = o_ref[:, cols - NGY :]


def merge(z, aux, up, dn):
    cols = z.shape[1]
    return pl.pallas_call(
        merge_kernel,
        out_shape=(
            jax.ShapeDtypeStruct((HALF, cols), F32),
            jax.ShapeDtypeStruct((HALF, NGY), F32),
            jax.ShapeDtypeStruct((HALF, NGY), F32),
        ),
        in_specs=vmem(4),
        out_specs=tuple(vmem(3)),
        cost_estimate=cost(4 * HALF * cols, 4 * HALF * cols * 4),
        name="merge",
    )(z, aux, up, dn)


def across_lanes(parts, coef, lo, hi):
    out = []
    for t in range(lo, hi):
        left, mid, right = parts[t], parts[t + 1], parts[t + 2]
        c = coef[:, t * NGY : (t + 1) * NGY]
        total = c[0:1] * mid
        if left is not None:
            total = total + c[1:2] * left
        if right is not None:
            total = total + c[2:3] * right
        total = total + c[3:4] * pltpu.roll(mid, 1, 1) + c[4:5] * pltpu.roll(mid, NGY - 1, 1)
        out.append(total)
    return out


def cols_kernel(z_ref, zl_ref, zr_ref, coef_ref, aux_ref, target_ref, x_ref, g_ref):
    cols = z_ref.shape[1]
    tiles = cols // NGY
    parts = [zl_ref[...]] + [z_ref[:, t * NGY : (t + 1) * NGY] for t in range(tiles)] + [zr_ref[...]]
    out = across_lanes(parts, coef_ref[...], 0, tiles)
    x = jnp.concatenate(out, axis=1)
    lane = lax.broadcasted_iota(jnp.int32, x.shape, 1)
    x = x + jnp.where(lane.astype(F32) == aux_ref[:, 3:4], aux_ref[:, 2:3], 0.0)
    x_ref[...] = x
    pick = lax.broadcasted_iota(jnp.int32, (cols, NGY), 0) == target_ref[...]
    g_ref[...] = jnp.dot(x, pick.astype(F32), precision=HI, preferred_element_type=F32)


def well_cols(z, zl, zr, coef, aux, target):
    cols = z.shape[1]
    return pl.pallas_call(
        cols_kernel,
        out_shape=(
            jax.ShapeDtypeStruct((HALF, cols), F32),
            jax.ShapeDtypeStruct((HALF, NGY), F32),
        ),
        in_specs=vmem(6),
        out_specs=tuple(vmem(2)),
        cost_estimate=cost(12 * HALF * cols * NGY, 4 * HALF * cols * 4),
        name="well_cols",
    )(z, zl, zr, coef, aux, target)


def left_tile(rc, mid, above, below):
    total = rc[0] * mid + rc[1] * above + rc[2] * below
    return total + rc[3] * pltpu.roll(mid, 1, 0) + rc[4] * pltpu.roll(mid, NGY - 1, 0)


BLK = 128
STEP = 4


def inverse_two(a, b, c):
    q = 1.0 / (a * c - b * b)
    return c * q, -b * q, a * q


def inverse_four(e):
    a, b, c = inverse_two(e[0][0], e[0][1], e[1][1])
    two = range(2)
    side = [[e[i][2 + k] for k in two] for i in two]
    w = [
        [a * side[0][k] + b * side[1][k] for k in two],
        [b * side[0][k] + c * side[1][k] for k in two],
    ]
    s = [
        [e[2 + i][2 + k] - (side[0][i] * w[0][k] + side[1][i] * w[1][k]) for k in two] for i in two
    ]
    p, q, t = inverse_two(s[0][0], s[0][1], s[1][1])
    v = [[w[i][0] * p + w[i][1] * q, w[i][0] * q + w[i][1] * t] for i in two]
    t00 = a + v[0][0] * w[0][0] + v[0][1] * w[0][1]
    t01 = b + v[0][0] * w[1][0] + v[0][1] * w[1][1]
    t11 = c + v[1][0] * w[1][0] + v[1][1] * w[1][1]
    return [
        [t00, t01, -v[0][0], -v[0][1]],
        [t01, t11, -v[1][0], -v[1][1]],
        [-v[0][0], -v[1][0], p, q],
        [-v[0][1], -v[1][1], q, t],
    ]


def small_inverse(d):
    size = d.shape[0]
    wide = (8, size)
    chunks = [d[8 * q : 8 * q + 8] for q in range(size // 8)]
    sub = lax.broadcasted_iota(jnp.int32, wide, 0)
    lane = lax.broadcasted_iota(jnp.int32, wide, 1)
    four = range(STEP)
    for j in range(0, size, STEP):
        home, o = divmod(j, 8)
        row = [jnp.broadcast_to(chunks[home][o + a : o + a + 1], wide) for a in four]
        e = [[None] * STEP for _ in four]
        for a in four:
            for b in range(a, STEP):
                e[a][b] = e[b][a] = jnp.broadcast_to(row[a][:, j + b : j + b + 1], wide)
        piv = inverse_four(e)
        inside = (lane >= j) & (lane < j + STEP)
        row = [jnp.where(lane == j + a, 1.0, jnp.where(inside, 0.0, row[a])) for a in four]
        new = [
            (piv[a][0] * row[0] + piv[a][1] * row[1]) + (piv[a][2] * row[2] + piv[a][3] * row[3])
            for a in four
        ]
        out = []
        for q, chunk in enumerate(chunks):
            col = [jnp.broadcast_to(chunk[:, j + a : j + a + 1], wide) for a in four]
            less = (col[0] * new[0] + col[1] * new[1]) + (col[2] * new[2] + col[3] * new[3])
            rest = jnp.where(inside, 0.0, chunk) - less
            if q == home:
                for a in four:
                    rest = jnp.where(sub == o + a, new[a], rest)
            out.append(rest)
        chunks = out
    return jnp.concatenate(chunks, axis=0)


def dot(a, b):
    return jnp.dot(a, b, precision=HI, preferred_element_type=F32)


def inverse_kernel(own_ref, other_ref, rslot_ref, cslot_ref, noise_ref, o_ref, s_ref):
    rows_in = ROWS * HALF
    pick_rows = (lax.broadcasted_iota(jnp.int32, (M, rows_in), 1) == rslot_ref[...]).astype(F32)
    total = jnp.zeros((M, M), F32)
    for k, ref in enumerate((own_ref, other_ref)):
        for h in range(2):
            piece = ref[:, h].reshape(rows_in, NGY)
            some = dot(pick_rows, piece)
            base = (2 * k + h) * NGY
            pick = lax.broadcasted_iota(jnp.int32, (NGY, M), 0) + base == cslot_ref[...]
            total = total + dot(some, pick.astype(F32))
    i0 = lax.broadcasted_iota(jnp.int32, (M, M), 0)
    i1 = lax.broadcasted_iota(jnp.int32, (M, M), 1)
    s_ref[...] = total + jnp.where(i0 == i1, noise_ref[...], 0.0)
    sub = lax.broadcasted_iota(jnp.int32, (M, BLK), 0)
    for b in range(M // BLK):
        lo = b * BLK
        inv = small_inverse(s_ref[lo : lo + BLK, lo : lo + BLK])
        panel = s_ref[lo : lo + BLK, :]
        col = s_ref[:, lo : lo + BLK]
        here = (i1[0:BLK] >= lo) & (i1[0:BLK] < lo + BLK)
        scaled = dot(inv, panel)
        inside = (sub >= lo) & (sub < lo + BLK)
        upd = dot(jnp.where(inside, 0.0, col), scaled)
        down = dot(col, inv)
        s_ref[...] = s_ref[...] - upd
        s_ref[:, lo : lo + BLK] = -down
        s_ref[lo : lo + BLK, :] = scaled
        s_ref[lo : lo + BLK, lo : lo + BLK] = inv
    o_ref[...] = s_ref[...]


def inverse(own, other, rslot, cslot, noise):
    return pl.pallas_call(
        inverse_kernel,
        out_shape=jax.ShapeDtypeStruct((M, M), F32),
        in_specs=vmem(5),
        out_specs=vmem(1)[0],
        scratch_shapes=[pltpu.VMEM((M, M), F32)],
        compiler_params=pltpu.CompilerParams(vmem_limit_bytes=10 << 20),
        cost_estimate=cost(2 * 1153000000 * 8, 4 << 20),
        name="inverse",
    )(own, other, rslot, cslot, noise)


def split(x):
    high = x.astype(BF16)
    return high, (x - high.astype(F32)).astype(BF16)


def bdot(a, b, dims=((1,), (0,))):
    return lax.dot_general(a, b, (dims, ((), ())), preferred_element_type=F32)


def three(x):
    high, low = split(x)
    return high, low, (x - high.astype(F32) - low.astype(F32)).astype(BF16)


def joined(refs):
    return jnp.concatenate([p[...].reshape(-1, p.shape[-1]) for p in refs], axis=0)


def across_kernel(slot_ref, *refs):
    pick = (lax.broadcasted_iota(jnp.int32, (M, SLOTS), 1) == slot_ref[...]).astype(BF16)
    high, mid, low = three(joined(refs[:-1]))
    refs[-1][...] = bdot(pick, high) + (bdot(pick, mid) + bdot(pick, low))


def across(slot, parts):
    cols = parts[0].shape[-1]
    return pl.pallas_call(
        across_kernel,
        out_shape=jax.ShapeDtypeStruct((M, cols), F32),
        in_specs=vmem(1 + len(parts)),
        out_specs=vmem(1)[0],
        compiler_params=pltpu.CompilerParams(vmem_limit_bytes=14 << 20),
        cost_estimate=cost(6 * M * SLOTS * cols, 3 * SLOTS * cols * 4),
        name="across",
    )(slot, *parts)


def strip_kernel(slot_ref, *refs):
    pick = (lax.broadcasted_iota(jnp.int32, (SLOTS, M), 0) == slot_ref[...]).astype(BF16)
    high, low = split(joined(refs[:-2]))
    refs[-2][...] = bdot(high, pick, ((0,), (0,))).astype(BF16)
    refs[-1][...] = bdot(low, pick, ((0,), (0,))).astype(BF16)


def strip(slot, parts):
    size = parts[0].shape[-1]
    return pl.pallas_call(
        strip_kernel,
        out_shape=(jax.ShapeDtypeStruct((size, M), BF16), jax.ShapeDtypeStruct((size, M), BF16)),
        in_specs=vmem(1 + len(parts)),
        out_specs=tuple(vmem(2)),
        compiler_params=pltpu.CompilerParams(vmem_limit_bytes=14 << 20),
        cost_estimate=cost(4 * M * SLOTS * size, 2 * SLOTS * size * 4),
        name="strip",
    )(slot, *parts)


def update_kernel(
    place, p_ref, proc_ref, inv_ref, xc_ref, rc_ref, cc_ref, up_ref, dn_ref, el_ref, er_ref,
    oh_ref, ol_ref, ph_ref, pl_ref, o_ref, uh, ul, sh, sl,
):
    h, j = pl.program_id(0), pl.program_id(1)
    steps = pl.num_programs(1)
    g = (h ^ place[0]) * steps + j
    final = 2 * steps - 1
    size, cols = o_ref.shape
    tiles, many = cols // NGY, size // NGY
    last = 2 * steps * many - 1

    @pl.when((h == 0) & (j == 0))
    def _():
        high, low = split(dot(inv_ref[...], xc_ref[...]))
        uh[...] = high
        ul[...] = low

    rows = pl.ds(pl.multiple_of(j * size, size), size)
    for half, (hi_ref, lo_ref) in enumerate(((oh_ref, ol_ref), (ph_ref, pl_ref))):

        @pl.when(h == half)
        def _():
            sh[...] = hi_ref[rows, :]
            sl[...] = lo_ref[rows, :]

    less = bdot(sh[...], uh[...]) + (bdot(sh[...], ul[...]) + bdot(sl[...], uh[...]))
    wide = (NGY, NGY)
    eye = lax.broadcasted_iota(jnp.int32, wide, 0) == lax.broadcasted_iota(jnp.int32, wide, 1)
    for n in range(many):
        k = g * many + n
        some = slice(n * NGY, (n + 1) * NGY)
        rc = [jnp.broadcast_to(rc_ref[some, i : i + 1], wide) for i in range(5)]
        inner = [rc[0], jnp.where(k == 0, 0.0, rc[1]), jnp.where(k == last, 0.0, rc[2]), rc[3], rc[4]]
        a, b, d = (pl.ds(pl.multiple_of((k + i) * NGY, NGY), NGY) for i in range(3))
        here = pl.ds(pl.multiple_of(k * NGY, NGY), NGY)
        above = pl.ds(pl.multiple_of(jnp.maximum(k - 1, 0) * NGY, NGY), NGY)
        below = pl.ds(pl.multiple_of(jnp.minimum(k + 1, last) * NGY, NGY), NGY)
        parts = [left_tile(rc, el_ref[b, :], el_ref[a, :], el_ref[d, :])]
        for t in range(tiles + 1):
            lanes = slice(t * NGY, (t + 1) * NGY)
            if t < tiles:
                parts.append(left_tile(inner, p_ref[here, lanes], p_ref[above, lanes], p_ref[below, lanes]))
            else:
                parts.append(left_tile(rc, er_ref[b, :], er_ref[a, :], er_ref[d, :]))
            if t >= 1:
                lanes = slice((t - 1) * NGY, t * NGY)
                o_ref[some, lanes] = across_lanes(parts, cc_ref[...], t - 1, t)[0] - less[some, lanes]
        hit = place[1] + k

        @pl.when((hit >= 0) & (hit < tiles))
        def _():
            lanes = pl.ds(pl.multiple_of(hit * NGY, NGY), NGY)
            o_ref[some, lanes] = o_ref[some, lanes] + jnp.where(eye, proc_ref[:, lanes], 0.0)

    for at, n, ref, k in ((0, 0, up_ref, 1), (final, many - 1, dn_ref, 2)):

        @pl.when(g == at)
        def _():
            some = slice(n * NGY, (n + 1) * NGY)
            scale = jnp.broadcast_to(rc_ref[some, k : k + 1], wide)
            parts = [None] + [scale * ref[:, t * NGY : (t + 1) * NGY] for t in range(tiles)] + [None]
            rim = across_lanes(parts, cc_ref[...], 0, tiles)
            o_ref[some, :] = o_ref[some, :] + jnp.concatenate(rim, axis=1)


def update(place, block, proc, inv, xc, row_coef, col_coef, rims, own, other):
    rows, cols = block.shape
    half = rows // 2
    size = 2 * NGY
    steps = half // size
    tile = pl.BlockSpec((size, cols), lambda h, j, k: ((h ^ k[0]) * steps + j, 0))
    few = pl.BlockSpec((size, 8), lambda h, j, k: ((h ^ k[0]) * steps + j, 0))
    return pl.pallas_call(
        update_kernel,
        out_shape=jax.ShapeDtypeStruct((rows, cols), F32),
        grid_spec=pltpu.PrefetchScalarGridSpec(
            num_scalar_prefetch=1,
            grid=(2, steps),
            in_specs=vmem(4) + [few] + vmem(9),
            out_specs=tile,
            scratch_shapes=[
                pltpu.VMEM((M, cols), BF16),
                pltpu.VMEM((M, cols), BF16),
                pltpu.VMEM((size, M), BF16),
                pltpu.VMEM((size, M), BF16),
            ],
        ),
        compiler_params=pltpu.CompilerParams(vmem_limit_bytes=30 << 20),
        cost_estimate=cost(6 * rows * cols * M, 8 * rows * cols),
        name="update",
    )(place, block, proc, inv, xc, row_coef, col_coef, *rims, *own, *other)


def shift(x, axis, count, back):
    return lax.ppermute(x, axis, [((i + back) % count, i) for i in range(count)])


def flip(x, axis, count, bit):
    return lax.ppermute(x, axis, [(i, i ^ bit) for i in range(count)])


def after(x, *others):
    return lax.optimization_barrier((x,) + others)[0]


def shards(covariance, center, links, process, wells, noise):
    r = lax.axis_index("row")
    c = lax.axis_index("col")
    rows, cols = covariance.shape
    cells = center.shape[0]
    row_start, col_start = r * rows, c * cols
    block = covariance

    z, send_up, send_dn, aux, target, top, low, left, right = tables(
        jnp.stack([r, c]), wells, center, links, process, block
    )
    got_up = shift(send_up, "row", ROWS, ROWS - 1)
    got_dn = shift(send_dn, "row", ROWS, 1)
    up = shift(low, "row", ROWS, ROWS - 1)
    z, to_left, to_right = merge(z, aux, got_up, got_dn)
    dn = shift(after(top, z), "row", ROWS, 1)
    zl = shift(to_right, "col", COLS, COLS - 1)
    zr = shift(to_left, "col", COLS, 1)

    cell = jnp.arange(cells, dtype=jnp.int32)
    gx, gy = cell // NGY, cell % NGY
    coef = jnp.concatenate(
        [
            center[None],
            jnp.where(gx == 0, 0.0, links[0])[None],
            jnp.where(gx == cells // NGY - 1, 0.0, links[1])[None],
            jnp.where(gy == 0, 0.0, links[2])[None],
            jnp.where(gy == NGY - 1, 0.0, links[3])[None],
            process[None],
        ]
    )
    coef = after(coef, send_dn)
    col_coef = lax.dynamic_slice_in_dim(coef, col_start, cols, 1)
    row_part = lax.dynamic_slice_in_dim(coef, row_start, rows, 1)
    start = ((row_start - col_start) // NGY)[None]
    row_coef = jnp.concatenate([row_part, jnp.zeros((2, rows), F32)]).T
    x, g = well_cols(z, zl, zr, col_coef[:5], aux, target)

    turn = []
    for z_at in range(4):
        for y in range(2):
            for q in range(ROWS):
                for k in range(2):
                    to = (((z_at + q // 2) % 4) * 2 + y) * 2 + k
                    turn.append(((z_at * 2 + y) * COLS + 2 * q + k, q * COLS + to))
    first = lax.ppermute(x, ("row", "col"), turn)
    mate = flip(x, "row", ROWS, 1)
    second = lax.ppermute(mate, ("row", "col"), turn)

    g = g + shift(g, "col", COLS, 4) + shift(g, "col", COLS, 8) + shift(g, "col", COLS, 12)
    g = after(g, mate, first, dn)
    g = jnp.stack([g, flip(g, "col", COLS, 2)])
    g = jnp.stack([g, flip(g, "row", ROWS, 1)])
    gated = g
    g = jnp.stack([g] + [shift(g, "row", ROWS, 2 * d) for d in range(1, 4)])
    g = g.reshape(ROWS, 2, HALF, NGY)
    g_other = flip(g, "col", COLS, 1)

    pair = after(jnp.stack([x, mate]), g)
    more = shift(pair, "row", ROWS, 2)
    less = shift(pair, "row", ROWS, ROWS - 2)
    x_parts = [pair, more, shift(more[0], "row", ROWS, 2), shift(less[1], "row", ROWS, ROWS - 2), less]
    pair = jnp.stack([first, second])
    more = shift(pair, "col", COLS, 4)
    less = shift(pair, "col", COLS, COLS - 4)
    far = shift(more[0], "col", COLS, 4), shift(less[1], "col", COLS, COLS - 4)
    own = [pair, more, *far, less]
    other = [flip(a, "col", COLS, 1) for a in (pair, jnp.stack([more, less]), jnp.stack(far))]
    other = [other[0], other[1][0], other[2], other[1][1]]

    def cornered(edge, lanes):
        edge = lax.dynamic_update_slice(edge, up[:, lanes], (0, 0))
        return lax.dynamic_update_slice(edge, dn[:, lanes], (rows + NGY, 0))

    el = shift(after(cornered(right, slice(cols - NGY, cols)), gated), "col", COLS, COLS - 1)
    er = shift(after(cornered(left, slice(0, NGY)), gated), "col", COLS, 1)

    w = after(wells, z)[0]
    part = w // cols
    number = jnp.arange(M, dtype=jnp.int32)
    same = (part[:, None] == part[None, :]) & (number[None, :] < number[:, None])
    rank = jnp.sum(same.astype(jnp.int32), axis=1)
    wr, wc = part // 2, part
    in_row = (wc % 2) * WMAX + rank
    row_slot = ((wr // 2 - r // 2) % 4 * 2 + (wr % 2 ^ r % 2)) * HALF + in_row
    gram_slot = ((wr // 2 - r // 2) % 4 * 2 + (wr % 2 ^ r % 2)) * HALF + in_row
    strip_slot = ((wr // 2 + r // 2 - c // 4) % 4 * 2 + (wr % 2 ^ (c // 2) % 2)) * HALF + in_row
    col_slot = (
        (wc % 2 ^ c % 2) * (2 * NGY)
        + ((wc // 2) % 2 ^ (c // 2) % 2) * NGY
        + (wc // 4) * WMAX
        + rank
    )
    xc = across(row_slot[:, None], x_parts)
    own = strip(strip_slot[None], own)
    other = strip(strip_slot[None], other)
    inv = inverse(g, g_other, gram_slot[:, None], col_slot[None], noise)
    rims = (up, dn, el, er)
    scalars = jnp.stack([c % 2, start[0]])
    return update(scalars, block, col_coef[5:6], inv, xc, row_coef, col_coef[:5], rims, own, other)


def solution(mesh):
    in_specs = (P("row", "col"), P(), P(), P(), P(), P())
    out_specs = P("row", "col")
    return jax.shard_map(shards, mesh=mesh, in_specs=in_specs, out_specs=out_specs, check_vma=False)
```

```python
import functools

import jax
import jax.numpy as jnp
from jax import lax
from jax.experimental import pallas as pl
from jax.experimental.pallas import tpu as pltpu
from jax.sharding import PartitionSpec as P

NGY = 128
M = 256
WMAX = 32
ROWS = 8
COLS = 16
HALF = 2 * WMAX
SLOTS = ROWS * HALF
F32 = jnp.float32
BF16 = jnp.bfloat16
HI = lax.Precision.HIGHEST


def cost(flops, size):
    return pl.CostEstimate(flops=flops, bytes_accessed=size, transcendentals=0)


def vmem(count):
    return [pl.BlockSpec(memory_space=pltpu.VMEM)] * count


def table_kernel(
    place, wells, center, links, process, block,
    z_ref, up_ref, dn_ref, aux_ref, target_ref, top_ref, low_ref, left_ref, right_ref,
    p_ref, own, side, noise, cell, count, sems,
):
    rows, cols = block.shape
    r, c = place[0], place[1]
    row_start, col_start = pl.multiple_of(r * rows, rows), c * cols
    part = pl.ds(row_start, rows)
    copies = [
        pltpu.make_async_copy(block.at[pl.ds(0, NGY)], top_ref, sems.at[0]),
        pltpu.make_async_copy(block.at[pl.ds(rows - NGY, NGY)], low_ref, sems.at[1]),
        pltpu.make_async_copy(center.at[part], own, sems.at[2]),
        pltpu.make_async_copy(links.at[:, part], side, sems.at[3]),
        pltpu.make_async_copy(process.at[part], noise, sems.at[4]),
        pltpu.make_async_copy(block, p_ref, sems.at[5]),
    ]
    for copy in copies:
        copy.start()

    for i in range(SLOTS // WMAX):
        count[i] = 0

    def none(i, carry):
        for k in range(16):
            cell[i * 16 + k] = -1
        return carry

    lax.fori_loop(0, SLOTS // 16, none, 0)
    shift_by = cols.bit_length() - 1

    def put(m, carry):
        w = wells[0, m]
        home = w >> shift_by
        n = count[home]
        cell[home * WMAX + n] = w
        count[home] = n + 1
        return carry

    lax.fori_loop(0, M, put, 0, unroll=16)
    for copy in copies:
        copy.wait()

    left_ref[NGY : rows + NGY, :] = p_ref[:, 0:NGY]
    right_ref[NGY : rows + NGY, :] = p_ref[:, cols - NGY :]
    lane = lax.broadcasted_iota(jnp.int32, (1, NGY), 1)

    def two(s, carry):
        up = cell[jnp.minimum((r + 1) * HALF + s, SLOTS - 1)] - NGY - row_start - (rows - NGY)
        dn = cell[jnp.maximum(r * HALF - WMAX + s, 0)] + NGY - row_start
        up_ref[pl.ds(s, 1), :] = low_ref[pl.ds(jnp.clip(up, 0, NGY - 1), 1), :]
        dn_ref[pl.ds(s, 1), :] = top_ref[pl.ds(jnp.clip(dn, 0, NGY - 1), 1), :]
        return carry

    lax.fori_loop(0, WMAX, two, 0, unroll=4)

    def one(s, carry):
        w = cell[r * HALF + s]
        good = w >= 0
        i = jnp.where(good, w - row_start, 0)
        first, final = i < NGY, i >= rows - NGY
        gy = i & (NGY - 1)
        gate = jnp.where(good, 1.0, 0.0)
        k1, k2 = side[0, i] * gate, side[1, i] * gate
        k3 = jnp.where(gy == 0, 0.0, side[2, i] * gate)
        k4 = jnp.where(gy == NGY - 1, 0.0, side[3, i] * gate)
        low, high = jnp.maximum(i - 1, 0), jnp.minimum(i + 1, rows - 1)
        above, below = jnp.maximum(i - NGY, 0), jnp.minimum(i + NGY, rows - 1)
        total = (own[i] * gate) * p_ref[pl.ds(i, 1), :]
        total = total + jnp.where(first, 0.0, k1) * p_ref[pl.ds(above, 1), :]
        total = total + jnp.where(final, 0.0, k2) * p_ref[pl.ds(below, 1), :]
        z_ref[pl.ds(s, 1), :] = total + k3 * p_ref[pl.ds(low, 1), :] + k4 * p_ref[pl.ds(high, 1), :]
        row = jnp.where(lane == 0, jnp.where(first & (r > 0), k1, 0.0), 0.0)
        row = jnp.where(lane == 1, jnp.where(final & (r < ROWS - 1), k2, 0.0), row)
        row = jnp.where(lane == 2, noise[i] * gate, row)
        col = jnp.where(good, w - col_start, -1)
        row = jnp.where(lane == 3, jnp.full((1, NGY), col, jnp.int32).astype(F32), row)
        aux_ref[pl.ds(s, 1), :] = row
        return carry

    lax.fori_loop(0, HALF, one, 0, unroll=4)
    base = (c // 4) * WMAX

    def three(t, row):
        return jnp.where(lane == base + t, cell[c * WMAX + t] - col_start, row)

    target_ref[...] = lax.fori_loop(0, WMAX, three, jnp.full((1, NGY), -1, jnp.int32), unroll=4)


def tables(place, wells, center, links, process, block):
    rows, cols = block.shape
    smem = pl.BlockSpec(memory_space=pltpu.SMEM)
    hbm = pl.BlockSpec(memory_space=pltpu.HBM)
    return pl.pallas_call(
        table_kernel,
        out_shape=(
            jax.ShapeDtypeStruct((HALF, cols), F32),
            jax.ShapeDtypeStruct((WMAX, cols), F32),
            jax.ShapeDtypeStruct((WMAX, cols), F32),
            jax.ShapeDtypeStruct((HALF, NGY), F32),
            jax.ShapeDtypeStruct((1, NGY), jnp.int32),
            jax.ShapeDtypeStruct((NGY, cols), F32),
            jax.ShapeDtypeStruct((NGY, cols), F32),
            jax.ShapeDtypeStruct((rows + 2 * NGY, NGY), F32),
            jax.ShapeDtypeStruct((rows + 2 * NGY, NGY), F32),
        ),
        in_specs=[smem, smem, hbm, hbm, hbm, hbm],
        out_specs=tuple(vmem(9)),
        scratch_shapes=[
            pltpu.VMEM((rows, cols), F32),
            pltpu.SMEM((rows,), F32),
            pltpu.SMEM((4, rows), F32),
            pltpu.SMEM((rows,), F32),
            pltpu.SMEM((SLOTS,), jnp.int32),
            pltpu.SMEM((SLOTS // WMAX,), jnp.int32),
            pltpu.SemaphoreType.DMA((6,)),
        ],
        compiler_params=pltpu.CompilerParams(vmem_limit_bytes=60 << 20),
        cost_estimate=cost(1 << 20, 2 << 20),
        name="tables",
    )(place, wells, center, links, process, block)


def merge_kernel(z_ref, aux_ref, up_ref, dn_ref, o_ref, left_ref, right_ref):
    cols = z_ref.shape[1]
    scale = aux_ref[...]
    o_ref[0:WMAX] = z_ref[0:WMAX] + scale[0:WMAX, 0:1] * up_ref[...]
    o_ref[WMAX:] = z_ref[WMAX:] + scale[WMAX:, 1:2] * dn_ref[...]
    left_ref[...] = o_ref[:, 0:NGY]
    right_ref[...] = o_ref[:, cols - NGY :]


def merge(z, aux, up, dn):
    cols = z.shape[1]
    return pl.pallas_call(
        merge_kernel,
        out_shape=(
            jax.ShapeDtypeStruct((HALF, cols), F32),
            jax.ShapeDtypeStruct((HALF, NGY), F32),
            jax.ShapeDtypeStruct((HALF, NGY), F32),
        ),
        in_specs=vmem(4),
        out_specs=tuple(vmem(3)),
        cost_estimate=cost(4 * HALF * cols, 4 * HALF * cols * 4),
        name="merge",
    )(z, aux, up, dn)


def across_lanes(parts, coef, lo, hi):
    out = []
    for t in range(lo, hi):
        left, mid, right = parts[t], parts[t + 1], parts[t + 2]
        c = coef[:, t * NGY : (t + 1) * NGY]
        total = c[0:1] * mid
        if left is not None:
            total = total + c[1:2] * left
        if right is not None:
            total = total + c[2:3] * right
        total = total + c[3:4] * pltpu.roll(mid, 1, 1) + c[4:5] * pltpu.roll(mid, NGY - 1, 1)
        out.append(total)
    return out


def cols_kernel(z_ref, zl_ref, zr_ref, coef_ref, aux_ref, target_ref, x_ref, g_ref):
    cols = z_ref.shape[1]
    tiles = cols // NGY
    parts = [zl_ref[...]] + [z_ref[:, t * NGY : (t + 1) * NGY] for t in range(tiles)] + [zr_ref[...]]
    out = across_lanes(parts, coef_ref[...], 0, tiles)
    x = jnp.concatenate(out, axis=1)
    lane = lax.broadcasted_iota(jnp.int32, x.shape, 1)
    x = x + jnp.where(lane.astype(F32) == aux_ref[:, 3:4], aux_ref[:, 2:3], 0.0)
    x_ref[...] = x
    pick = lax.broadcasted_iota(jnp.int32, (cols, NGY), 0) == target_ref[...]
    g_ref[...] = jnp.dot(x, pick.astype(F32), precision=HI, preferred_element_type=F32)


def well_cols(z, zl, zr, coef, aux, target):
    cols = z.shape[1]
    return pl.pallas_call(
        cols_kernel,
        out_shape=(
            jax.ShapeDtypeStruct((HALF, cols), F32),
            jax.ShapeDtypeStruct((HALF, NGY), F32),
        ),
        in_specs=vmem(6),
        out_specs=tuple(vmem(2)),
        cost_estimate=cost(12 * HALF * cols * NGY, 4 * HALF * cols * 4),
        name="well_cols",
    )(z, zl, zr, coef, aux, target)


def left_tile(rc, mid, above, below):
    total = rc[0] * mid + rc[1] * above + rc[2] * below
    return total + rc[3] * pltpu.roll(mid, 1, 0) + rc[4] * pltpu.roll(mid, NGY - 1, 0)


BLK = 128
STEP = 4


def inverse_two(a, b, c):
    q = 1.0 / (a * c - b * b)
    return c * q, -b * q, a * q


def inverse_four(e):
    a, b, c = inverse_two(e[0][0], e[0][1], e[1][1])
    two = range(2)
    side = [[e[i][2 + k] for k in two] for i in two]
    w = [
        [a * side[0][k] + b * side[1][k] for k in two],
        [b * side[0][k] + c * side[1][k] for k in two],
    ]
    s = [
        [e[2 + i][2 + k] - (side[0][i] * w[0][k] + side[1][i] * w[1][k]) for k in two] for i in two
    ]
    p, q, t = inverse_two(s[0][0], s[0][1], s[1][1])
    v = [[w[i][0] * p + w[i][1] * q, w[i][0] * q + w[i][1] * t] for i in two]
    t00 = a + v[0][0] * w[0][0] + v[0][1] * w[0][1]
    t01 = b + v[0][0] * w[1][0] + v[0][1] * w[1][1]
    t11 = c + v[1][0] * w[1][0] + v[1][1] * w[1][1]
    return [
        [t00, t01, -v[0][0], -v[0][1]],
        [t01, t11, -v[1][0], -v[1][1]],
        [-v[0][0], -v[1][0], p, q],
        [-v[0][1], -v[1][1], q, t],
    ]


def small_inverse(d):
    size = d.shape[0]
    wide = (8, size)
    chunks = [d[8 * q : 8 * q + 8] for q in range(size // 8)]
    sub = lax.broadcasted_iota(jnp.int32, wide, 0)
    lane = lax.broadcasted_iota(jnp.int32, wide, 1)
    four = range(STEP)
    for j in range(0, size, STEP):
        home, o = divmod(j, 8)
        row = [jnp.broadcast_to(chunks[home][o + a : o + a + 1], wide) for a in four]
        e = [[None] * STEP for _ in four]
        for a in four:
            for b in range(a, STEP):
                e[a][b] = e[b][a] = jnp.broadcast_to(row[a][:, j + b : j + b + 1], wide)
        piv = inverse_four(e)
        inside = (lane >= j) & (lane < j + STEP)
        row = [jnp.where(lane == j + a, 1.0, jnp.where(inside, 0.0, row[a])) for a in four]
        new = [
            (piv[a][0] * row[0] + piv[a][1] * row[1]) + (piv[a][2] * row[2] + piv[a][3] * row[3])
            for a in four
        ]
        out = []
        for q, chunk in enumerate(chunks):
            col = [jnp.broadcast_to(chunk[:, j + a : j + a + 1], wide) for a in four]
            less = (col[0] * new[0] + col[1] * new[1]) + (col[2] * new[2] + col[3] * new[3])
            rest = jnp.where(inside, 0.0, chunk) - less
            if q == home:
                for a in four:
                    rest = jnp.where(sub == o + a, new[a], rest)
            out.append(rest)
        chunks = out
    return jnp.concatenate(chunks, axis=0)


def dot(a, b):
    return jnp.dot(a, b, precision=HI, preferred_element_type=F32)


def sum_of(parts):
    return parts[0] + (parts[1] + parts[2])


def inverse_kernel(own_ref, other_ref, rslot_ref, cslot_ref, noise_ref, o_ref, s_ref):
    rows_in = ROWS * HALF
    pick_rows = (lax.broadcasted_iota(jnp.int32, (M, rows_in), 1) == rslot_ref[...]).astype(BF16)
    pieces = [ref[:, h].reshape(rows_in, NGY) for ref in (own_ref, other_ref) for h in range(2)]
    some = sum_of([bdot(pick_rows, part) for part in three(jnp.concatenate(pieces, axis=1))])
    pick = (lax.broadcasted_iota(jnp.int32, (4 * NGY, M), 0) == cslot_ref[...]).astype(BF16)
    total = sum_of([bdot(part, pick) for part in three(some)])
    i0 = lax.broadcasted_iota(jnp.int32, (M, M), 0)
    i1 = lax.broadcasted_iota(jnp.int32, (M, M), 1)
    s_ref[...] = total + jnp.where(i0 == i1, noise_ref[...], 0.0)
    sub = lax.broadcasted_iota(jnp.int32, (M, BLK), 0)
    for b in range(M // BLK):
        lo = b * BLK
        inv = small_inverse(s_ref[lo : lo + BLK, lo : lo + BLK])
        panel = s_ref[lo : lo + BLK, :]
        col = s_ref[:, lo : lo + BLK]
        here = (i1[0:BLK] >= lo) & (i1[0:BLK] < lo + BLK)
        scaled = dot(inv, panel)
        inside = (sub >= lo) & (sub < lo + BLK)
        upd = dot(jnp.where(inside, 0.0, col), scaled)
        down = dot(col, inv)
        s_ref[...] = s_ref[...] - upd
        s_ref[:, lo : lo + BLK] = -down
        s_ref[lo : lo + BLK, :] = scaled
        s_ref[lo : lo + BLK, lo : lo + BLK] = inv
    o_ref[...] = s_ref[...]


def inverse(own, other, rslot, cslot, noise):
    return pl.pallas_call(
        inverse_kernel,
        out_shape=jax.ShapeDtypeStruct((M, M), F32),
        in_specs=vmem(5),
        out_specs=vmem(1)[0],
        scratch_shapes=[pltpu.VMEM((M, M), F32)],
        compiler_params=pltpu.CompilerParams(vmem_limit_bytes=10 << 20),
        cost_estimate=cost(2 * 1153000000 * 8, 4 << 20),
        name="inverse",
    )(own, other, rslot, cslot, noise)


def split(x):
    high = x.astype(BF16)
    return high, (x - high.astype(F32)).astype(BF16)


def bdot(a, b, dims=((1,), (0,))):
    return lax.dot_general(a, b, (dims, ((), ())), preferred_element_type=F32)


def three(x):
    high, low = split(x)
    return high, low, (x - high.astype(F32) - low.astype(F32)).astype(BF16)


def joined(refs):
    return jnp.concatenate([p[...].reshape(-1, p.shape[-1]) for p in refs], axis=0)


def across_kernel(slot_ref, inv_ref, *refs):
    pick = (lax.broadcasted_iota(jnp.int32, (M, SLOTS), 1) == slot_ref[...]).astype(BF16)
    rows = sum_of([bdot(pick, part) for part in three(joined(refs[:-2]))])
    high, low = split(dot(inv_ref[...], rows))
    refs[-2][...] = high
    refs[-1][...] = low


def across(slot, inv, parts):
    cols = parts[0].shape[-1]
    return pl.pallas_call(
        across_kernel,
        out_shape=(jax.ShapeDtypeStruct((M, cols), BF16), jax.ShapeDtypeStruct((M, cols), BF16)),
        in_specs=vmem(2 + len(parts)),
        out_specs=tuple(vmem(2)),
        compiler_params=pltpu.CompilerParams(vmem_limit_bytes=16 << 20),
        cost_estimate=cost(6 * M * SLOTS * cols, 3 * SLOTS * cols * 4),
        name="across",
    )(slot, inv, *parts)


def strip_kernel(slot_ref, *refs):
    pick = (lax.broadcasted_iota(jnp.int32, (SLOTS, M), 0) == slot_ref[...]).astype(BF16)
    high, low = split(joined(refs[:-2]))
    refs[-2][...] = bdot(high, pick, ((0,), (0,))).astype(BF16)
    refs[-1][...] = bdot(low, pick, ((0,), (0,))).astype(BF16)


def strip(slot, parts):
    size = parts[0].shape[-1]
    return pl.pallas_call(
        strip_kernel,
        out_shape=(jax.ShapeDtypeStruct((size, M), BF16), jax.ShapeDtypeStruct((size, M), BF16)),
        in_specs=vmem(1 + len(parts)),
        out_specs=tuple(vmem(2)),
        compiler_params=pltpu.CompilerParams(vmem_limit_bytes=14 << 20),
        cost_estimate=cost(4 * M * SLOTS * size, 2 * SLOTS * size * 4),
        name="strip",
    )(slot, *parts)


def update_kernel(
    place, p_ref, proc_ref, uh, ul, rc_ref, cc_ref, up_ref, dn_ref, el_ref, er_ref,
    oh_ref, ol_ref, ph_ref, pl_ref, o_ref, sh, sl,
):
    h, j = pl.program_id(0), pl.program_id(1)
    steps = pl.num_programs(1)
    g = (h ^ place[0]) * steps + j
    final = 2 * steps - 1
    size, cols = o_ref.shape
    tiles, many = cols // NGY, size // NGY
    last = 2 * steps * many - 1

    rows = pl.ds(pl.multiple_of(j * size, size), size)
    for half, (hi_ref, lo_ref) in enumerate(((oh_ref, ol_ref), (ph_ref, pl_ref))):

        @pl.when(h == half)
        def _():
            sh[...] = hi_ref[rows, :]
            sl[...] = lo_ref[rows, :]

    less = bdot(sh[...], uh[...]) + (bdot(sh[...], ul[...]) + bdot(sl[...], uh[...]))
    wide = (NGY, NGY)
    eye = lax.broadcasted_iota(jnp.int32, wide, 0) == lax.broadcasted_iota(jnp.int32, wide, 1)
    for n in range(many):
        k = g * many + n
        some = slice(n * NGY, (n + 1) * NGY)
        rc = [jnp.broadcast_to(rc_ref[some, i : i + 1], wide) for i in range(5)]
        inner = [rc[0], jnp.where(k == 0, 0.0, rc[1]), jnp.where(k == last, 0.0, rc[2]), rc[3], rc[4]]
        a, b, d = (pl.ds(pl.multiple_of((k + i) * NGY, NGY), NGY) for i in range(3))
        here = pl.ds(pl.multiple_of(k * NGY, NGY), NGY)
        above = pl.ds(pl.multiple_of(jnp.maximum(k - 1, 0) * NGY, NGY), NGY)
        below = pl.ds(pl.multiple_of(jnp.minimum(k + 1, last) * NGY, NGY), NGY)
        parts = [left_tile(rc, el_ref[b, :], el_ref[a, :], el_ref[d, :])]
        for t in range(tiles + 1):
            lanes = slice(t * NGY, (t + 1) * NGY)
            if t < tiles:
                parts.append(left_tile(inner, p_ref[here, lanes], p_ref[above, lanes], p_ref[below, lanes]))
            else:
                parts.append(left_tile(rc, er_ref[b, :], er_ref[a, :], er_ref[d, :]))
            if t >= 1:
                lanes = slice((t - 1) * NGY, t * NGY)
                o_ref[some, lanes] = across_lanes(parts, cc_ref[...], t - 1, t)[0] - less[some, lanes]
        hit = place[1] + k

        @pl.when((hit >= 0) & (hit < tiles))
        def _():
            lanes = pl.ds(pl.multiple_of(hit * NGY, NGY), NGY)
            o_ref[some, lanes] = o_ref[some, lanes] + jnp.where(eye, proc_ref[:, lanes], 0.0)

    for at, n, ref, k in ((0, 0, up_ref, 1), (final, many - 1, dn_ref, 2)):

        @pl.when(g == at)
        def _():
            some = slice(n * NGY, (n + 1) * NGY)
            scale = jnp.broadcast_to(rc_ref[some, k : k + 1], wide)
            parts = [None] + [scale * ref[:, t * NGY : (t + 1) * NGY] for t in range(tiles)] + [None]
            rim = across_lanes(parts, cc_ref[...], 0, tiles)
            o_ref[some, :] = o_ref[some, :] + jnp.concatenate(rim, axis=1)


def update(place, block, proc, solved, row_coef, col_coef, rims, own, other):
    rows, cols = block.shape
    half = rows // 2
    size = 2 * NGY
    steps = half // size
    tile = pl.BlockSpec((size, cols), lambda h, j, k: ((h ^ k[0]) * steps + j, 0))
    few = pl.BlockSpec((size, 8), lambda h, j, k: ((h ^ k[0]) * steps + j, 0))
    return pl.pallas_call(
        update_kernel,
        out_shape=jax.ShapeDtypeStruct((rows, cols), F32),
        grid_spec=pltpu.PrefetchScalarGridSpec(
            num_scalar_prefetch=1,
            grid=(2, steps),
            in_specs=vmem(4) + [few] + vmem(9),
            out_specs=tile,
            scratch_shapes=[
                pltpu.VMEM((size, M), BF16),
                pltpu.VMEM((size, M), BF16),
            ],
        ),
        compiler_params=pltpu.CompilerParams(vmem_limit_bytes=30 << 20),
        cost_estimate=cost(6 * rows * cols * M, 8 * rows * cols),
        name="update",
    )(place, block, proc, *solved, row_coef, col_coef, *rims, *own, *other)


def shift(x, axis, count, back):
    return lax.ppermute(x, axis, [((i + back) % count, i) for i in range(count)])


def flip(x, axis, count, bit):
    return lax.ppermute(x, axis, [(i, i ^ bit) for i in range(count)])


def after(x, *others):
    return lax.optimization_barrier((x,) + others)[0]


def shards(covariance, center, links, process, wells, noise):
    r = lax.axis_index("row")
    c = lax.axis_index("col")
    rows, cols = covariance.shape
    cells = center.shape[0]
    row_start, col_start = r * rows, c * cols
    block = covariance

    z, send_up, send_dn, aux, target, top, low, left, right = tables(
        jnp.stack([r, c]), wells, center, links, process, block
    )
    got_up = shift(send_up, "row", ROWS, ROWS - 1)
    got_dn = shift(send_dn, "row", ROWS, 1)
    up = shift(low, "row", ROWS, ROWS - 1)
    z, to_left, to_right = merge(z, aux, got_up, got_dn)
    dn = shift(after(top, z), "row", ROWS, 1)
    zl = shift(to_right, "col", COLS, COLS - 1)
    zr = shift(to_left, "col", COLS, 1)

    cell = jnp.arange(cells, dtype=jnp.int32)
    gx, gy = cell // NGY, cell % NGY
    coef = jnp.concatenate(
        [
            center[None],
            jnp.where(gx == 0, 0.0, links[0])[None],
            jnp.where(gx == cells // NGY - 1, 0.0, links[1])[None],
            jnp.where(gy == 0, 0.0, links[2])[None],
            jnp.where(gy == NGY - 1, 0.0, links[3])[None],
            process[None],
        ]
    )
    coef = after(coef, send_dn)
    col_coef = lax.dynamic_slice_in_dim(coef, col_start, cols, 1)
    row_part = lax.dynamic_slice_in_dim(coef, row_start, rows, 1)
    start = ((row_start - col_start) // NGY)[None]
    row_coef = jnp.concatenate([row_part, jnp.zeros((2, rows), F32)]).T
    x, g = well_cols(z, zl, zr, col_coef[:5], aux, target)

    turn = []
    for z_at in range(4):
        for y in range(2):
            for q in range(ROWS):
                for k in range(2):
                    to = (((z_at + q // 2) % 4) * 2 + y) * 2 + k
                    turn.append(((z_at * 2 + y) * COLS + 2 * q + k, q * COLS + to))
    first = lax.ppermute(x, ("row", "col"), turn)
    mate = flip(x, "row", ROWS, 1)
    second = lax.ppermute(mate, ("row", "col"), turn)

    g = g + shift(g, "col", COLS, 4) + shift(g, "col", COLS, 8) + shift(g, "col", COLS, 12)
    g = after(g, mate, first, dn)
    g = jnp.stack([g, flip(g, "col", COLS, 2)])
    g = jnp.stack([g, flip(g, "row", ROWS, 1)])
    gated = g
    g = jnp.stack([g] + [shift(g, "row", ROWS, 2 * d) for d in range(1, 4)])
    g = g.reshape(ROWS, 2, HALF, NGY)
    g_other = flip(g, "col", COLS, 1)

    pair = after(jnp.stack([x, mate]), g)
    more = shift(pair, "row", ROWS, 2)
    less = shift(pair, "row", ROWS, ROWS - 2)
    x_parts = [pair, more, shift(more[0], "row", ROWS, 2), shift(less[1], "row", ROWS, ROWS - 2), less]
    pair = jnp.stack([first, second])
    more = shift(pair, "col", COLS, 4)
    less = shift(pair, "col", COLS, COLS - 4)
    far = shift(more[0], "col", COLS, 4), shift(less[1], "col", COLS, COLS - 4)
    own = [pair, more, *far, less]
    other = [flip(a, "col", COLS, 1) for a in (pair, jnp.stack([more, less]), jnp.stack(far))]
    other = [other[0], other[1][0], other[2], other[1][1]]

    def cornered(edge, lanes):
        edge = lax.dynamic_update_slice(edge, up[:, lanes], (0, 0))
        return lax.dynamic_update_slice(edge, dn[:, lanes], (rows + NGY, 0))

    el = shift(after(cornered(right, slice(cols - NGY, cols)), gated), "col", COLS, COLS - 1)
    er = shift(after(cornered(left, slice(0, NGY)), gated), "col", COLS, 1)

    w = after(wells, z)[0]
    part = w // cols
    number = jnp.arange(M, dtype=jnp.int32)
    same = (part[:, None] == part[None, :]) & (number[None, :] < number[:, None])
    rank = jnp.sum(same.astype(jnp.int32), axis=1)
    wr, wc = part // 2, part
    in_row = (wc % 2) * WMAX + rank
    row_slot = ((wr // 2 - r // 2) % 4 * 2 + (wr % 2 ^ r % 2)) * HALF + in_row
    gram_slot = ((wr // 2 - r // 2) % 4 * 2 + (wr % 2 ^ r % 2)) * HALF + in_row
    strip_slot = ((wr // 2 + r // 2 - c // 4) % 4 * 2 + (wr % 2 ^ (c // 2) % 2)) * HALF + in_row
    col_slot = (
        (wc % 2 ^ c % 2) * (2 * NGY)
        + ((wc // 2) % 2 ^ (c // 2) % 2) * NGY
        + (wc // 4) * WMAX
        + rank
    )
    own = strip(strip_slot[None], own)
    other = strip(strip_slot[None], other)
    inv = inverse(g, g_other, gram_slot[:, None], col_slot[None], noise)
    solved = across(row_slot[:, None], inv, x_parts)
    rims = (up, dn, el, er)
    scalars = jnp.stack([c % 2, start[0]])
    return update(scalars, block, col_coef[5:6], solved, row_coef, col_coef[:5], rims, own, other)


def solution(mesh):
    in_specs = (P("row", "col"), P(), P(), P(), P(), P())
    out_specs = P("row", "col")
    return jax.shard_map(shards, mesh=mesh, in_specs=in_specs, out_specs=out_specs, check_vma=False)
```

```python
import functools

import jax
import jax.numpy as jnp
from jax import lax
from jax.experimental import pallas as pl
from jax.experimental.pallas import tpu as pltpu
from jax.sharding import PartitionSpec as P

NGY = 128
M = 256
WMAX = 32
ROWS = 8
COLS = 16
HALF = 2 * WMAX
SLOTS = ROWS * HALF
F32 = jnp.float32
BF16 = jnp.bfloat16
HI = lax.Precision.HIGHEST


def cost(flops, size):
    return pl.CostEstimate(flops=flops, bytes_accessed=size, transcendentals=0)


def vmem(count):
    return [pl.BlockSpec(memory_space=pltpu.VMEM)] * count


def table_kernel(
    place, wells, center, links, process, block,
    z_ref, up_ref, dn_ref, aux_ref, target_ref, top_ref, low_ref, left_ref, right_ref,
    p_ref, own, side, noise, cell, count, sems,
):
    rows, cols = block.shape
    r, c = place[0], place[1]
    row_start, col_start = pl.multiple_of(r * rows, rows), c * cols
    part = pl.ds(row_start, rows)
    copies = [
        pltpu.make_async_copy(block.at[pl.ds(0, NGY)], top_ref, sems.at[0]),
        pltpu.make_async_copy(block.at[pl.ds(rows - NGY, NGY)], low_ref, sems.at[1]),
        pltpu.make_async_copy(center.at[part], own, sems.at[2]),
        pltpu.make_async_copy(links.at[:, part], side, sems.at[3]),
        pltpu.make_async_copy(process.at[part], noise, sems.at[4]),
        pltpu.make_async_copy(block, p_ref, sems.at[5]),
    ]
    for copy in copies:
        copy.start()

    for i in range(SLOTS // WMAX):
        count[i] = 0

    def none(i, carry):
        for k in range(16):
            cell[i * 16 + k] = -1
        return carry

    lax.fori_loop(0, SLOTS // 16, none, 0)
    shift_by = cols.bit_length() - 1

    def put(m, carry):
        w = wells[0, m]
        home = w >> shift_by
        n = count[home]
        cell[home * WMAX + n] = w
        count[home] = n + 1
        return carry

    lax.fori_loop(0, M, put, 0, unroll=64)
    for copy in copies:
        copy.wait()

    left_ref[NGY : rows + NGY, :] = p_ref[:, 0:NGY]
    right_ref[NGY : rows + NGY, :] = p_ref[:, cols - NGY :]
    lane = lax.broadcasted_iota(jnp.int32, (1, NGY), 1)

    def two(s, carry):
        up = cell[jnp.minimum((r + 1) * HALF + s, SLOTS - 1)] - NGY - row_start - (rows - NGY)
        dn = cell[jnp.maximum(r * HALF - WMAX + s, 0)] + NGY - row_start
        up_ref[pl.ds(s, 1), :] = low_ref[pl.ds(jnp.clip(up, 0, NGY - 1), 1), :]
        dn_ref[pl.ds(s, 1), :] = top_ref[pl.ds(jnp.clip(dn, 0, NGY - 1), 1), :]
        return carry

    lax.fori_loop(0, WMAX, two, 0, unroll=4)

    def one(s, carry):
        w = cell[r * HALF + s]
        good = w >= 0
        i = jnp.where(good, w - row_start, 0)
        first, final = i < NGY, i >= rows - NGY
        gy = i & (NGY - 1)
        gate = jnp.where(good, 1.0, 0.0)
        k1, k2 = side[0, i] * gate, side[1, i] * gate
        k3 = jnp.where(gy == 0, 0.0, side[2, i] * gate)
        k4 = jnp.where(gy == NGY - 1, 0.0, side[3, i] * gate)
        low, high = jnp.maximum(i - 1, 0), jnp.minimum(i + 1, rows - 1)
        above, below = jnp.maximum(i - NGY, 0), jnp.minimum(i + NGY, rows - 1)
        total = (own[i] * gate) * p_ref[pl.ds(i, 1), :]
        total = total + jnp.where(first, 0.0, k1) * p_ref[pl.ds(above, 1), :]
        total = total + jnp.where(final, 0.0, k2) * p_ref[pl.ds(below, 1), :]
        z_ref[pl.ds(s, 1), :] = total + k3 * p_ref[pl.ds(low, 1), :] + k4 * p_ref[pl.ds(high, 1), :]
        row = jnp.where(lane == 0, jnp.where(first & (r > 0), k1, 0.0), 0.0)
        row = jnp.where(lane == 1, jnp.where(final & (r < ROWS - 1), k2, 0.0), row)
        row = jnp.where(lane == 2, noise[i] * gate, row)
        col = jnp.where(good, w - col_start, -1)
        row = jnp.where(lane == 3, jnp.full((1, NGY), col, jnp.int32).astype(F32), row)
        aux_ref[pl.ds(s, 1), :] = row
        return carry

    lax.fori_loop(0, HALF, one, 0, unroll=8)
    base = (c // 4) * WMAX

    def three(t, row):
        return jnp.where(lane == base + t, cell[c * WMAX + t] - col_start, row)

    target_ref[...] = lax.fori_loop(0, WMAX, three, jnp.full((1, NGY), -1, jnp.int32), unroll=4)


def tables(place, wells, center, links, process, block):
    rows, cols = block.shape
    smem = pl.BlockSpec(memory_space=pltpu.SMEM)
    hbm = pl.BlockSpec(memory_space=pltpu.HBM)
    return pl.pallas_call(
        table_kernel,
        out_shape=(
            jax.ShapeDtypeStruct((HALF, cols), F32),
            jax.ShapeDtypeStruct((WMAX, cols), F32),
            jax.ShapeDtypeStruct((WMAX, cols), F32),
            jax.ShapeDtypeStruct((HALF, NGY), F32),
            jax.ShapeDtypeStruct((1, NGY), jnp.int32),
            jax.ShapeDtypeStruct((NGY, cols), F32),
            jax.ShapeDtypeStruct((NGY, cols), F32),
            jax.ShapeDtypeStruct((rows + 2 * NGY, NGY), F32),
            jax.ShapeDtypeStruct((rows + 2 * NGY, NGY), F32),
        ),
        in_specs=[smem, smem, hbm, hbm, hbm, hbm],
        out_specs=tuple(vmem(9)),
        scratch_shapes=[
            pltpu.VMEM((rows, cols), F32),
            pltpu.SMEM((rows,), F32),
            pltpu.SMEM((4, rows), F32),
            pltpu.SMEM((rows,), F32),
            pltpu.SMEM((SLOTS,), jnp.int32),
            pltpu.SMEM((SLOTS // WMAX,), jnp.int32),
            pltpu.SemaphoreType.DMA((6,)),
        ],
        compiler_params=pltpu.CompilerParams(vmem_limit_bytes=60 << 20),
        cost_estimate=cost(1 << 20, 2 << 20),
        name="tables",
    )(place, wells, center, links, process, block)


def merge_kernel(z_ref, aux_ref, up_ref, dn_ref, o_ref, left_ref, right_ref):
    cols = z_ref.shape[1]
    scale = aux_ref[...]
    o_ref[0:WMAX] = z_ref[0:WMAX] + scale[0:WMAX, 0:1] * up_ref[...]
    o_ref[WMAX:] = z_ref[WMAX:] + scale[WMAX:, 1:2] * dn_ref[...]
    left_ref[...] = o_ref[:, 0:NGY]
    right_ref[...] = o_ref[:, cols - NGY :]


def merge(z, aux, up, dn):
    cols = z.shape[1]
    return pl.pallas_call(
        merge_kernel,
        out_shape=(
            jax.ShapeDtypeStruct((HALF, cols), F32),
            jax.ShapeDtypeStruct((HALF, NGY), F32),
            jax.ShapeDtypeStruct((HALF, NGY), F32),
        ),
        in_specs=vmem(4),
        out_specs=tuple(vmem(3)),
        cost_estimate=cost(4 * HALF * cols, 4 * HALF * cols * 4),
        name="merge",
    )(z, aux, up, dn)


def across_lanes(parts, coef, lo, hi):
    out = []
    for t in range(lo, hi):
        left, mid, right = parts[t], parts[t + 1], parts[t + 2]
        c = coef[:, t * NGY : (t + 1) * NGY]
        total = c[0:1] * mid
        if left is not None:
            total = total + c[1:2] * left
        if right is not None:
            total = total + c[2:3] * right
        total = total + c[3:4] * pltpu.roll(mid, 1, 1) + c[4:5] * pltpu.roll(mid, NGY - 1, 1)
        out.append(total)
    return out


def cols_kernel(z_ref, zl_ref, zr_ref, coef_ref, aux_ref, target_ref, x_ref, g_ref):
    cols = z_ref.shape[1]
    tiles = cols // NGY
    parts = [zl_ref[...]] + [z_ref[:, t * NGY : (t + 1) * NGY] for t in range(tiles)] + [zr_ref[...]]
    out = across_lanes(parts, coef_ref[...], 0, tiles)
    x = jnp.concatenate(out, axis=1)
    lane = lax.broadcasted_iota(jnp.int32, x.shape, 1)
    x = x + jnp.where(lane.astype(F32) == aux_ref[:, 3:4], aux_ref[:, 2:3], 0.0)
    x_ref[...] = x
    pick = lax.broadcasted_iota(jnp.int32, (cols, NGY), 0) == target_ref[...]
    pick = pick.astype(BF16)
    g_ref[...] = sum_of([bdot(part, pick) for part in three(x)])


def well_cols(z, zl, zr, coef, aux, target):
    cols = z.shape[1]
    return pl.pallas_call(
        cols_kernel,
        out_shape=(
            jax.ShapeDtypeStruct((HALF, cols), F32),
            jax.ShapeDtypeStruct((HALF, NGY), F32),
        ),
        in_specs=vmem(6),
        out_specs=tuple(vmem(2)),
        cost_estimate=cost(12 * HALF * cols * NGY, 4 * HALF * cols * 4),
        name="well_cols",
    )(z, zl, zr, coef, aux, target)


def left_tile(rc, mid, above, below):
    total = rc[0] * mid + rc[1] * above + rc[2] * below
    return total + rc[3] * pltpu.roll(mid, 1, 0) + rc[4] * pltpu.roll(mid, NGY - 1, 0)


BLK = 128
STEP = 4


def inverse_two(a, b, c):
    q = 1.0 / (a * c - b * b)
    return c * q, -b * q, a * q


def inverse_four(e):
    a, b, c = inverse_two(e[0][0], e[0][1], e[1][1])
    two = range(2)
    side = [[e[i][2 + k] for k in two] for i in two]
    w = [
        [a * side[0][k] + b * side[1][k] for k in two],
        [b * side[0][k] + c * side[1][k] for k in two],
    ]
    s = [
        [e[2 + i][2 + k] - (side[0][i] * w[0][k] + side[1][i] * w[1][k]) for k in two] for i in two
    ]
    p, q, t = inverse_two(s[0][0], s[0][1], s[1][1])
    v = [[w[i][0] * p + w[i][1] * q, w[i][0] * q + w[i][1] * t] for i in two]
    t00 = a + v[0][0] * w[0][0] + v[0][1] * w[0][1]
    t01 = b + v[0][0] * w[1][0] + v[0][1] * w[1][1]
    t11 = c + v[1][0] * w[1][0] + v[1][1] * w[1][1]
    return [
        [t00, t01, -v[0][0], -v[0][1]],
        [t01, t11, -v[1][0], -v[1][1]],
        [-v[0][0], -v[1][0], p, q],
        [-v[0][1], -v[1][1], q, t],
    ]


def small_inverse(d):
    size = d.shape[0]
    wide = (8, size)
    chunks = [d[8 * q : 8 * q + 8] for q in range(size // 8)]
    sub = lax.broadcasted_iota(jnp.int32, wide, 0)
    lane = lax.broadcasted_iota(jnp.int32, wide, 1)
    four = range(STEP)
    for j in range(0, size, STEP):
        home, o = divmod(j, 8)
        row = [jnp.broadcast_to(chunks[home][o + a : o + a + 1], wide) for a in four]
        e = [[None] * STEP for _ in four]
        for a in four:
            for b in range(a, STEP):
                e[a][b] = e[b][a] = jnp.broadcast_to(row[a][:, j + b : j + b + 1], wide)
        piv = inverse_four(e)
        inside = (lane >= j) & (lane < j + STEP)
        row = [jnp.where(lane == j + a, 1.0, jnp.where(inside, 0.0, row[a])) for a in four]
        new = [
            (piv[a][0] * row[0] + piv[a][1] * row[1]) + (piv[a][2] * row[2] + piv[a][3] * row[3])
            for a in four
        ]
        out = []
        for q, chunk in enumerate(chunks):
            col = [jnp.broadcast_to(chunk[:, j + a : j + a + 1], wide) for a in four]
            less = (col[0] * new[0] + col[1] * new[1]) + (col[2] * new[2] + col[3] * new[3])
            rest = jnp.where(inside, 0.0, chunk) - less
            if q == home:
                for a in four:
                    rest = jnp.where(sub == o + a, new[a], rest)
            out.append(rest)
        chunks = out
    return jnp.concatenate(chunks, axis=0)


def dot(a, b):
    return jnp.dot(a, b, precision=HI, preferred_element_type=F32)


def sum_of(parts):
    return parts[0] + (parts[1] + parts[2])


def inverse_kernel(own_ref, other_ref, rslot_ref, cslot_ref, noise_ref, o_ref, s_ref):
    rows_in = ROWS * HALF
    pick_rows = (lax.broadcasted_iota(jnp.int32, (M, rows_in), 1) == rslot_ref[...]).astype(BF16)
    pieces = [ref[:, h].reshape(rows_in, NGY) for ref in (own_ref, other_ref) for h in range(2)]
    some = sum_of([bdot(pick_rows, part) for part in three(jnp.concatenate(pieces, axis=1))])
    pick = (lax.broadcasted_iota(jnp.int32, (4 * NGY, M), 0) == cslot_ref[...]).astype(BF16)
    total = sum_of([bdot(part, pick) for part in three(some)])
    i0 = lax.broadcasted_iota(jnp.int32, (M, M), 0)
    i1 = lax.broadcasted_iota(jnp.int32, (M, M), 1)
    s_ref[...] = total + jnp.where(i0 == i1, noise_ref[...], 0.0)
    sub = lax.broadcasted_iota(jnp.int32, (M, BLK), 0)
    for b in range(M // BLK):
        lo = b * BLK
        inv = small_inverse(s_ref[lo : lo + BLK, lo : lo + BLK])
        panel = s_ref[lo : lo + BLK, :]
        col = s_ref[:, lo : lo + BLK]
        here = (i1[0:BLK] >= lo) & (i1[0:BLK] < lo + BLK)
        scaled = dot(inv, panel)
        inside = (sub >= lo) & (sub < lo + BLK)
        upd = dot(jnp.where(inside, 0.0, col), scaled)
        down = dot(col, inv)
        s_ref[...] = s_ref[...] - upd
        s_ref[:, lo : lo + BLK] = -down
        s_ref[lo : lo + BLK, :] = scaled
        s_ref[lo : lo + BLK, lo : lo + BLK] = inv
    o_ref[...] = s_ref[...]


def inverse(own, other, rslot, cslot, noise):
    return pl.pallas_call(
        inverse_kernel,
        out_shape=jax.ShapeDtypeStruct((M, M), F32),
        in_specs=vmem(5),
        out_specs=vmem(1)[0],
        scratch_shapes=[pltpu.VMEM((M, M), F32)],
        compiler_params=pltpu.CompilerParams(vmem_limit_bytes=10 << 20),
        cost_estimate=cost(2 * 1153000000 * 8, 4 << 20),
        name="inverse",
    )(own, other, rslot, cslot, noise)


def split(x):
    high = x.astype(BF16)
    return high, (x - high.astype(F32)).astype(BF16)


def bdot(a, b, dims=((1,), (0,))):
    return lax.dot_general(a, b, (dims, ((), ())), preferred_element_type=F32)


def three(x):
    high, low = split(x)
    return high, low, (x - high.astype(F32) - low.astype(F32)).astype(BF16)


def joined(refs):
    return jnp.concatenate([p[...].reshape(-1, p.shape[-1]) for p in refs], axis=0)


def across_kernel(slot_ref, inv_ref, *refs):
    pick = (lax.broadcasted_iota(jnp.int32, (M, SLOTS), 1) == slot_ref[...]).astype(BF16)
    rows = sum_of([bdot(pick, part) for part in three(joined(refs[:-2]))])
    high, low = split(dot(inv_ref[...], rows))
    refs[-2][...] = high
    refs[-1][...] = low


def across(slot, inv, parts):
    cols = parts[0].shape[-1]
    return pl.pallas_call(
        across_kernel,
        out_shape=(jax.ShapeDtypeStruct((M, cols), BF16), jax.ShapeDtypeStruct((M, cols), BF16)),
        in_specs=vmem(2 + len(parts)),
        out_specs=tuple(vmem(2)),
        compiler_params=pltpu.CompilerParams(vmem_limit_bytes=16 << 20),
        cost_estimate=cost(6 * M * SLOTS * cols, 3 * SLOTS * cols * 4),
        name="across",
    )(slot, inv, *parts)


def strip_kernel(slot_ref, *refs):
    pick = (lax.broadcasted_iota(jnp.int32, (SLOTS, M), 0) == slot_ref[...]).astype(BF16)
    high, low = split(joined(refs[:-2]))
    refs[-2][...] = bdot(high, pick, ((0,), (0,))).astype(BF16)
    refs[-1][...] = bdot(low, pick, ((0,), (0,))).astype(BF16)


def strip(slot, parts):
    size = parts[0].shape[-1]
    return pl.pallas_call(
        strip_kernel,
        out_shape=(jax.ShapeDtypeStruct((size, M), BF16), jax.ShapeDtypeStruct((size, M), BF16)),
        in_specs=vmem(1 + len(parts)),
        out_specs=tuple(vmem(2)),
        compiler_params=pltpu.CompilerParams(vmem_limit_bytes=14 << 20),
        cost_estimate=cost(4 * M * SLOTS * size, 2 * SLOTS * size * 4),
        name="strip",
    )(slot, *parts)


def update_kernel(
    place, p_ref, proc_ref, uh, ul, rc_ref, cc_ref, up_ref, dn_ref, el_ref, er_ref,
    oh_ref, ol_ref, ph_ref, pl_ref, o_ref, sh, sl,
):
    h, j = pl.program_id(0), pl.program_id(1)
    steps = pl.num_programs(1)
    g = (h ^ place[0]) * steps + j
    final = 2 * steps - 1
    size, cols = o_ref.shape
    tiles, many = cols // NGY, size // NGY
    last = 2 * steps * many - 1

    rows = pl.ds(pl.multiple_of(j * size, size), size)
    for half, (hi_ref, lo_ref) in enumerate(((oh_ref, ol_ref), (ph_ref, pl_ref))):

        @pl.when(h == half)
        def _():
            sh[...] = hi_ref[rows, :]
            sl[...] = lo_ref[rows, :]

    less = bdot(sh[...], uh[...]) + (bdot(sh[...], ul[...]) + bdot(sl[...], uh[...]))
    wide = (NGY, NGY)
    eye = lax.broadcasted_iota(jnp.int32, wide, 0) == lax.broadcasted_iota(jnp.int32, wide, 1)
    for n in range(many):
        k = g * many + n
        some = slice(n * NGY, (n + 1) * NGY)
        rc = [jnp.broadcast_to(rc_ref[some, i : i + 1], wide) for i in range(5)]
        inner = [rc[0], jnp.where(k == 0, 0.0, rc[1]), jnp.where(k == last, 0.0, rc[2]), rc[3], rc[4]]
        a, b, d = (pl.ds(pl.multiple_of((k + i) * NGY, NGY), NGY) for i in range(3))
        here = pl.ds(pl.multiple_of(k * NGY, NGY), NGY)
        above = pl.ds(pl.multiple_of(jnp.maximum(k - 1, 0) * NGY, NGY), NGY)
        below = pl.ds(pl.multiple_of(jnp.minimum(k + 1, last) * NGY, NGY), NGY)
        parts = [left_tile(rc, el_ref[b, :], el_ref[a, :], el_ref[d, :])]
        for t in range(tiles + 1):
            lanes = slice(t * NGY, (t + 1) * NGY)
            if t < tiles:
                parts.append(left_tile(inner, p_ref[here, lanes], p_ref[above, lanes], p_ref[below, lanes]))
            else:
                parts.append(left_tile(rc, er_ref[b, :], er_ref[a, :], er_ref[d, :]))
            if t >= 1:
                lanes = slice((t - 1) * NGY, t * NGY)
                o_ref[some, lanes] = across_lanes(parts, cc_ref[...], t - 1, t)[0] - less[some, lanes]
        hit = place[1] + k

        @pl.when((hit >= 0) & (hit < tiles))
        def _():
            lanes = pl.ds(pl.multiple_of(hit * NGY, NGY), NGY)
            o_ref[some, lanes] = o_ref[some, lanes] + jnp.where(eye, proc_ref[:, lanes], 0.0)

    for at, n, ref, k in ((0, 0, up_ref, 1), (final, many - 1, dn_ref, 2)):

        @pl.when(g == at)
        def _():
            some = slice(n * NGY, (n + 1) * NGY)
            scale = jnp.broadcast_to(rc_ref[some, k : k + 1], wide)
            parts = [None] + [scale * ref[:, t * NGY : (t + 1) * NGY] for t in range(tiles)] + [None]
            rim = across_lanes(parts, cc_ref[...], 0, tiles)
            o_ref[some, :] = o_ref[some, :] + jnp.concatenate(rim, axis=1)


def update(place, block, proc, solved, row_coef, col_coef, rims, own, other):
    rows, cols = block.shape
    half = rows // 2
    size = 2 * NGY
    steps = half // size
    tile = pl.BlockSpec((size, cols), lambda h, j, k: ((h ^ k[0]) * steps + j, 0))
    few = pl.BlockSpec((size, 8), lambda h, j, k: ((h ^ k[0]) * steps + j, 0))
    return pl.pallas_call(
        update_kernel,
        out_shape=jax.ShapeDtypeStruct((rows, cols), F32),
        grid_spec=pltpu.PrefetchScalarGridSpec(
            num_scalar_prefetch=1,
            grid=(2, steps),
            in_specs=vmem(4) + [few] + vmem(9),
            out_specs=tile,
            scratch_shapes=[
                pltpu.VMEM((size, M), BF16),
                pltpu.VMEM((size, M), BF16),
            ],
        ),
        compiler_params=pltpu.CompilerParams(vmem_limit_bytes=30 << 20),
        cost_estimate=cost(6 * rows * cols * M, 8 * rows * cols),
        name="update",
    )(place, block, proc, *solved, row_coef, col_coef, *rims, *own, *other)


def shift(x, axis, count, back):
    return lax.ppermute(x, axis, [((i + back) % count, i) for i in range(count)])


def flip(x, axis, count, bit):
    return lax.ppermute(x, axis, [(i, i ^ bit) for i in range(count)])


def after(x, *others):
    return lax.optimization_barrier((x,) + others)[0]


def shards(covariance, center, links, process, wells, noise):
    r = lax.axis_index("row")
    c = lax.axis_index("col")
    rows, cols = covariance.shape
    cells = center.shape[0]
    row_start, col_start = r * rows, c * cols
    block = covariance

    z, send_up, send_dn, aux, target, top, low, left, right = tables(
        jnp.stack([r, c]), wells, center, links, process, block
    )
    got_up = shift(send_up, "row", ROWS, ROWS - 1)
    got_dn = shift(send_dn, "row", ROWS, 1)
    up = shift(low, "row", ROWS, ROWS - 1)
    z, to_left, to_right = merge(z, aux, got_up, got_dn)
    dn = shift(after(top, z), "row", ROWS, 1)
    zl = shift(to_right, "col", COLS, COLS - 1)
    zr = shift(to_left, "col", COLS, 1)

    cell = jnp.arange(cells, dtype=jnp.int32)
    gx, gy = cell // NGY, cell % NGY
    coef = jnp.concatenate(
        [
            center[None],
            jnp.where(gx == 0, 0.0, links[0])[None],
            jnp.where(gx == cells // NGY - 1, 0.0, links[1])[None],
            jnp.where(gy == 0, 0.0, links[2])[None],
            jnp.where(gy == NGY - 1, 0.0, links[3])[None],
            process[None],
        ]
    )
    coef = after(coef, send_dn)
    col_coef = lax.dynamic_slice_in_dim(coef, col_start, cols, 1)
    row_part = lax.dynamic_slice_in_dim(coef, row_start, rows, 1)
    start = ((row_start - col_start) // NGY)[None]
    row_coef = jnp.concatenate([row_part, jnp.zeros((2, rows), F32)]).T
    x, g = well_cols(z, zl, zr, col_coef[:5], aux, target)

    turn = []
    for z_at in range(4):
        for y in range(2):
            for q in range(ROWS):
                for k in range(2):
                    to = (((z_at + q // 2) % 4) * 2 + y) * 2 + k
                    turn.append(((z_at * 2 + y) * COLS + 2 * q + k, q * COLS + to))
    first = lax.ppermute(x, ("row", "col"), turn)
    mate = flip(x, "row", ROWS, 1)
    second = lax.ppermute(mate, ("row", "col"), turn)

    g = g + shift(g, "col", COLS, 4) + shift(g, "col", COLS, 8) + shift(g, "col", COLS, 12)
    g = after(g, mate, first, dn)
    g = jnp.stack([g, flip(g, "col", COLS, 2)])
    g = jnp.stack([g, flip(g, "row", ROWS, 1)])
    gated = g
    g = jnp.stack([g] + [shift(g, "row", ROWS, 2 * d) for d in range(1, 4)])
    g = g.reshape(ROWS, 2, HALF, NGY)
    g_other = flip(g, "col", COLS, 1)

    pair = after(jnp.stack([x, mate]), g)
    more = shift(pair, "row", ROWS, 2)
    less = shift(pair, "row", ROWS, ROWS - 2)
    x_parts = [pair, more, shift(more[0], "row", ROWS, 2), shift(less[1], "row", ROWS, ROWS - 2), less]
    pair = jnp.stack([first, second])
    more = shift(pair, "col", COLS, 4)
    less = shift(pair, "col", COLS, COLS - 4)
    far = shift(more[0], "col", COLS, 4), shift(less[1], "col", COLS, COLS - 4)
    own = [pair, more, *far, less]
    other = [flip(a, "col", COLS, 1) for a in (pair, jnp.stack([more, less]), jnp.stack(far))]
    other = [other[0], other[1][0], other[2], other[1][1]]

    def cornered(edge, lanes):
        edge = lax.dynamic_update_slice(edge, up[:, lanes], (0, 0))
        return lax.dynamic_update_slice(edge, dn[:, lanes], (rows + NGY, 0))

    el = shift(after(cornered(right, slice(cols - NGY, cols)), gated), "col", COLS, COLS - 1)
    er = shift(after(cornered(left, slice(0, NGY)), gated), "col", COLS, 1)

    w = after(wells, z)[0]
    part = w // cols
    number = jnp.arange(M, dtype=jnp.int32)
    same = (part[:, None] == part[None, :]) & (number[None, :] < number[:, None])
    rank = jnp.sum(same.astype(jnp.int32), axis=1)
    wr, wc = part // 2, part
    in_row = (wc % 2) * WMAX + rank
    row_slot = ((wr // 2 - r // 2) % 4 * 2 + (wr % 2 ^ r % 2)) * HALF + in_row
    gram_slot = ((wr // 2 - r // 2) % 4 * 2 + (wr % 2 ^ r % 2)) * HALF + in_row
    strip_slot = ((wr // 2 + r // 2 - c // 4) % 4 * 2 + (wr % 2 ^ (c // 2) % 2)) * HALF + in_row
    col_slot = (
        (wc % 2 ^ c % 2) * (2 * NGY)
        + ((wc // 2) % 2 ^ (c // 2) % 2) * NGY
        + (wc // 4) * WMAX
        + rank
    )
    own = strip(strip_slot[None], own)
    other = strip(strip_slot[None], other)
    inv = inverse(g, g_other, gram_slot[:, None], col_slot[None], noise)
    solved = across(row_slot[:, None], inv, x_parts)
    rims = (up, dn, el, er)
    scalars = jnp.stack([c % 2, start[0]])
    return update(scalars, block, col_coef[5:6], solved, row_coef, col_coef[:5], rims, own, other)


def solution(mesh):
    in_specs = (P("row", "col"), P(), P(), P(), P(), P())
    out_specs = P("row", "col")
    return jax.shard_map(shards, mesh=mesh, in_specs=in_specs, out_specs=out_specs, check_vma=False)
```
